512 devices in a mesh: row: 128 (over y, z, core), col: 4 (over x).
Axes of the slice: x: 4, y: 4, z: 16, core: 2. Of those that a mesh axis runs over, the one named last changes fastest.
Arguments:
- residual: float32 [65536, 128], P('row'), may hold values from -6 to 6
- solution: float32 [65536, 128], P('row'), may hold values from -6 to 6
- near_field_blocks: float32 [256, 4, 256, 256], P('row', 'col'), may hold values from -0.09375 to 0.09375
- near_cols: int32 [256, 4], P('row', 'col'), may hold values from 0 to 255, as said below
- couplings: float32 [256, 64, 16, 16], P('row', 'col'), may hold values from -0.1875 to 0.1875
- far_cols: int32 [256, 64], P('row', 'col'), may hold values from 0 to 255, as said below
- far_count: int32 [256], P('row'), may hold values from 16 to 64, as said below
- col_basis: float32 [256, 16, 256], P('row'), may hold values from -0.375 to 0.375
- row_basis: float32 [256, 16, 256], P('row'), may hold values from -0.75 to 0.75
Outputs:
- solution_next: float32 [65536, 128], P('row')
- hessenberg: float32 [5, 4, 128], replicated
The draws below stay inside these ranges and needn't reach their ends.
Inputs may be any that keep to these rules, and one draw needn't show every extreme that they name: near_cols[i, 0] = i; the other entries of row cluster i are i + t for distinct nonzero t with |t| <= 2, clipped to 0 .. 255. far_cols[i, p] differs from i by more than 2, counted around the ends of the cluster range. Slots p >= far_count[i] of row cluster i are unused; some row cluster uses all 64 slots.
All inputs are finite; a program needn't handle non-finite values.
Results may differ from the reference program's by a relative error of at most 0.0001.
Values sent between devices are 32-bit elements; how exact they have to be, the bound alone decides.
A program may use at most 64 MiB of HBM per device.

```python
import jax
import jax.numpy as jnp
from jax import lax

LEAF_UNKNOWNS = 256
K = 16
RHS = 128
NEAR_BLOCK_COUNT = 4
REACH = 2
FAR = 64
SB = 4
LEAF_COUNT = 256
N = 65536


def draw_near_cols(key, part):
    cluster_ids = jnp.arange(LEAF_COUNT, dtype=jnp.int32)
    option_n = 2 * REACH
    scores = jax.random.randint(key, (LEAF_COUNT, option_n), 0, 1 << 20) * option_n + jnp.arange(option_n, dtype=jnp.int32)[None, :]
    cluster_ranking = jnp.argsort(scores, axis=1)
    every_offset = jnp.concatenate([-jnp.arange(REACH, 0, -1, dtype=jnp.int32), jnp.arange(1, REACH + 1, dtype=jnp.int32)])
    basis_shifts = jnp.take(every_offset, cluster_ranking[:, :NEAR_BLOCK_COUNT - 1], axis=0)
    others = jnp.clip(cluster_ids[:, None] + basis_shifts, 0, LEAF_COUNT - 1)
    return jnp.concatenate([cluster_ids[:, None], others], axis=1).astype(jnp.int32)


def draw_far_cols(key, part):
    cluster_ids = jnp.arange(LEAF_COUNT, dtype=jnp.int32)
    offsets = jax.random.randint(key, (LEAF_COUNT, FAR), 0, LEAF_COUNT - 2 * REACH - 1)
    return ((cluster_ids[:, None] + REACH + 1 + offsets) % LEAF_COUNT).astype(jnp.int32)


def draw_far_count(key, part):
    first_key, second_key, third_key = jax.random.split(key, 3)
    counts = jax.random.randint(first_key, (LEAF_COUNT,), FAR // 4, FAR + 1)
    fullest = jax.random.randint(second_key, (), 0, LEAF_COUNT)
    sparse_at = (fullest + 1 + jax.random.randint(third_key, (), 0, LEAF_COUNT - 1)) % LEAF_COUNT
    return counts.at[fullest].set(FAR).at[sparse_at].set(FAR // 4).astype(jnp.int32)


def block_levels(stream_key, extent, cuts, least, high):
    gain = 1.0
    for dim, shards_of in cuts:
        draws = jax.random.uniform(jax.random.fold_in(jax.random.fold_in(stream_key, 6), dim), (shards_of,), jnp.float32, least / len(cuts), high / len(cuts))
        gain = gain * jnp.repeat(jnp.exp(draws), extent[dim] // shards_of).reshape((-1,) + (1,) * (len(extent) - 1 - dim))
    return gain


def gaussian(stream_key, extent, scale, most, cuts=(), kind=jnp.bfloat16):
    array = scale * jax.random.normal(stream_key, extent, jnp.float32)
    if cuts:
        array = array * block_levels(stream_key, extent, cuts, -0.22, 0.18)
    return jnp.clip(array, -most, most).astype(kind)


def setup_inputs(seed: int = 0) -> dict:
    streams_of = jax.random.split(jax.random.key(seed), 10)
    residual = gaussian(streams_of[0], (N, RHS), 1.0, 6.0, ((0, 128),), jnp.float32)
    solution = gaussian(streams_of[1], (N, RHS), 1.0, 6.0, ((0, 128),), jnp.float32)
    near_field_blocks = gaussian(streams_of[2], (LEAF_COUNT, NEAR_BLOCK_COUNT, LEAF_UNKNOWNS, LEAF_UNKNOWNS), (4 * NEAR_BLOCK_COUNT * LEAF_UNKNOWNS) ** -0.5, 0.09375, ((0, 128), (1, 4)), jnp.float32)
    near_cols = draw_near_cols(jax.random.fold_in(streams_of[9], 71), 0)
    couplings = gaussian(streams_of[4], (LEAF_COUNT, FAR, K, K), (FAR * K) ** -0.5, 0.1875, ((0, 128), (1, 4)), jnp.float32)
    far_cols = draw_far_cols(jax.random.fold_in(streams_of[9], 71), 0)
    far_count = draw_far_count(jax.random.fold_in(streams_of[9], 71), 0)
    col_basis = gaussian(streams_of[7], (LEAF_COUNT, K, LEAF_UNKNOWNS), LEAF_UNKNOWNS ** -0.5, 0.375, ((0, 128),), jnp.float32)
    row_basis = gaussian(streams_of[8], (LEAF_COUNT, K, LEAF_UNKNOWNS), (4 * K) ** -0.5, 0.75, ((0, 128),), jnp.float32)
    return dict(residual=residual, solution=solution, near_field_blocks=near_field_blocks, near_cols=near_cols, couplings=couplings, far_cols=far_cols, far_count=far_count, col_basis=col_basis, row_basis=row_basis)


HIGH = lax.Precision.HIGHEST
SHIFT = 1.0

def cholesky_upper(entries, order_n):
    zero_entry = jnp.zeros_like(entries[0][0])
    upper_r = []
    for row_idx in range(order_n):
        upper_r.append([zero_entry] * order_n)
    for row_idx in range(order_n):
        running = entries[row_idx][row_idx]
        for earlier in range(row_idx):
            running = running - upper_r[earlier][row_idx] * upper_r[earlier][row_idx]
        pivot_val = jnp.sqrt(running)
        upper_r[row_idx][row_idx] = pivot_val
        for col_idx in range(row_idx + 1, order_n):
            entry_val = entries[row_idx][col_idx]
            for earlier in range(row_idx):
                entry_val = entry_val - upper_r[earlier][row_idx] * upper_r[earlier][col_idx]
            upper_r[row_idx][col_idx] = entry_val / pivot_val
    return upper_r

def small_update(gram_sum, scale_factor, depth_n):
    order_n = depth_n + 1
    entries = [[gram_sum[row_idx, col_idx] for col_idx in range(order_n)] for row_idx in range(order_n)]
    upper_r = cholesky_upper(entries, order_n)
    shifted = [[SHIFT * upper_r[row_idx][col_idx] + upper_r[row_idx][col_idx + 1] for col_idx in range(depth_n)] for row_idx in range(order_n)]
    hessen = []
    for row_idx in range(order_n):
        row_vals = []
        for col_idx in range(depth_n):
            entry_val = shifted[row_idx][col_idx]
            for earlier in range(col_idx):
                entry_val = entry_val - row_vals[earlier] * upper_r[earlier][col_idx]
            row_vals.append(entry_val / upper_r[col_idx][col_idx])
        hessen.append(row_vals)
    normal = []
    for row_idx in range(depth_n):
        row_vals = []
        for col_idx in range(depth_n):
            entry_val = hessen[0][row_idx] * hessen[0][col_idx]
            for inner in range(1, order_n):
                entry_val = entry_val + hessen[inner][row_idx] * hessen[inner][col_idx]
            row_vals.append(entry_val)
        normal.append(row_vals)
    target = [scale_factor * upper_r[0][0] * hessen[0][col_idx] for col_idx in range(depth_n)]
    factor = cholesky_upper(normal, depth_n)
    forward = []
    for row_idx in range(depth_n):
        entry_val = target[row_idx]
        for earlier in range(row_idx):
            entry_val = entry_val - factor[earlier][row_idx] * forward[earlier]
        forward.append(entry_val / factor[row_idx][row_idx])
    solved = [None] * depth_n
    for row_idx in range(depth_n - 1, -1, -1):
        entry_val = forward[row_idx]
        for later in range(row_idx + 1, depth_n):
            entry_val = entry_val - factor[row_idx][later] * solved[later]
        solved[row_idx] = entry_val / factor[row_idx][row_idx]
    weights = [None] * depth_n
    for row_idx in range(depth_n - 1, -1, -1):
        entry_val = solved[row_idx]
        for later in range(row_idx + 1, depth_n):
            entry_val = entry_val - upper_r[row_idx][later] * weights[later]
        weights[row_idx] = entry_val / upper_r[row_idx][row_idx]
    hess_array = jnp.stack([jnp.stack(hessen[row_idx], 0) for row_idx in range(order_n)], 0)
    return (hess_array, weights)

def reference(residual, solution, near_field_blocks, near_cols, couplings, far_cols, far_count, col_basis, row_basis):
    live_mask = (jnp.arange(FAR, dtype=jnp.int32)[None, :] < far_count[:, None]).astype(jnp.float32)
    weighted = couplings * live_mask[:, :, None, None]

    def apply_operator(vectors):
        panels = vectors.reshape(LEAF_COUNT, LEAF_UNKNOWNS, RHS)
        picked = jnp.take(panels, near_cols.astype(jnp.int32), axis=0)
        near_part = jnp.einsum('csab,csbr->car', near_field_blocks, picked, precision=HIGH)
        coeffs = jnp.einsum('ckb,cbr->ckr', col_basis, panels, precision=HIGH)
        fetched = jnp.take(coeffs, far_cols.astype(jnp.int32), axis=0)
        summed = jnp.einsum('cfkl,cflr->ckr', weighted, fetched, precision=HIGH)
        far_part = jnp.einsum('ckb,ckr->cbr', row_basis, summed, precision=HIGH)
        return (near_part + far_part).reshape(LEAF_COUNT * LEAF_UNKNOWNS, RHS)
    basis_list = [residual]
    current = residual
    for step_k in range(SB):
        current = apply_operator(current)
        basis_list.append(current)
    stacked = jnp.stack(basis_list, 0)
    gram_sum = jnp.einsum('anr,bnr->abr', stacked, stacked, precision=HIGH)
    hessenberg, weights = small_update(gram_sum, jnp.ones((RHS,), jnp.float32), SB)
    solution_next = solution
    for step_k in range(SB):
        solution_next = solution_next + weights[step_k][None, :] * basis_list[step_k]
    return (solution_next, hessenberg)
```

```python
import functools

import jax
import jax.numpy as jnp
from jax import lax
from jax.experimental import pallas as pl
from jax.experimental.pallas import tpu as pltpu
from jax.sharding import PartitionSpec as P

LEAF_UNKNOWNS = 256
CL_DEV = 2
REACH = 2
SB = 4
RANK = 16
LANES = 128
NY, NZ, NC = 4, 16, 2
NX = 4
NROW = NY * NZ * NC
WIDTH = LANES // NX
ROWS = CL_DEV * LEAF_UNKNOWNS
SLOTS = 16
FAR = SLOTS * NX
PAIRS = [(a, b) for a in range(SB + 1) for b in range(a, SB + 1)]


HIGH = lax.Precision.HIGHEST
SHIFT = 1.0
MESH = pl.DeviceIdType.MESH


def cholesky_upper(entries, order_n):
    zero_entry = jnp.zeros_like(entries[0][0])
    upper_r = []
    for row_idx in range(order_n):
        upper_r.append([zero_entry] * order_n)
    for row_idx in range(order_n):
        running = entries[row_idx][row_idx]
        for earlier in range(row_idx):
            running = running - upper_r[earlier][row_idx] * upper_r[earlier][row_idx]
        pivot_val = jnp.sqrt(running)
        upper_r[row_idx][row_idx] = pivot_val
        for col_idx in range(row_idx + 1, order_n):
            entry_val = entries[row_idx][col_idx]
            for earlier in range(row_idx):
                entry_val = entry_val - upper_r[earlier][row_idx] * upper_r[earlier][col_idx]
            upper_r[row_idx][col_idx] = entry_val / pivot_val
    return upper_r


def small_update(gram_sum, scale_factor, depth_n):
    order_n = depth_n + 1
    entries = gram_sum
    upper_r = cholesky_upper(entries, order_n)
    shifted = [
        [
            SHIFT * upper_r[row_idx][col_idx] + upper_r[row_idx][col_idx + 1]
            for col_idx in range(depth_n)
        ]
        for row_idx in range(order_n)
    ]
    hessen = []
    for row_idx in range(order_n):
        row_vals = []
        for col_idx in range(depth_n):
            entry_val = shifted[row_idx][col_idx]
            for earlier in range(col_idx):
                entry_val = entry_val - row_vals[earlier] * upper_r[earlier][col_idx]
            row_vals.append(entry_val / upper_r[col_idx][col_idx])
        hessen.append(row_vals)
    normal = []
    for row_idx in range(depth_n):
        row_vals = []
        for col_idx in range(depth_n):
            entry_val = hessen[0][row_idx] * hessen[0][col_idx]
            for inner in range(1, order_n):
                entry_val = entry_val + hessen[inner][row_idx] * hessen[inner][col_idx]
            row_vals.append(entry_val)
        normal.append(row_vals)
    target = [scale_factor * upper_r[0][0] * hessen[0][col_idx] for col_idx in range(depth_n)]
    factor = cholesky_upper(normal, depth_n)
    forward = []
    for row_idx in range(depth_n):
        entry_val = target[row_idx]
        for earlier in range(row_idx):
            entry_val = entry_val - factor[earlier][row_idx] * forward[earlier]
        forward.append(entry_val / factor[row_idx][row_idx])
    solved = [None] * depth_n
    for row_idx in range(depth_n - 1, -1, -1):
        entry_val = forward[row_idx]
        for later in range(row_idx + 1, depth_n):
            entry_val = entry_val - factor[row_idx][later] * solved[later]
        solved[row_idx] = entry_val / factor[row_idx][row_idx]
    weights = [None] * depth_n
    for row_idx in range(depth_n - 1, -1, -1):
        entry_val = solved[row_idx]
        for later in range(row_idx + 1, depth_n):
            entry_val = entry_val - upper_r[row_idx][later] * weights[later]
        weights[row_idx] = entry_val / upper_r[row_idx][row_idx]
    return (hessen, weights)


def dot(left, right):
    return jnp.dot(left, right, precision=HIGH, preferred_element_type=jnp.float32)


def lane_group(shape):
    return lax.broadcasted_iota(jnp.int32, shape, 1) // WIDTH


def pack(pieces):
    group = lane_group(pieces[0].shape)
    out = pieces[0]
    for q in range(1, len(pieces)):
        out = jnp.where(group == q, pltpu.roll(pieces[q], q * WIDTH, 1), out)
    return out


def lanes_to_front(value, q):
    return value if q == 0 else pltpu.roll(value, LANES - q * WIDTH, 1)


def kernel(
    idx, res, sol, near, coup, cb, rbt, out, hout,
    W, T, U, HP, HB, H, F, NB, CP, GR, GZ, GY, GC, XO, XH,
    z_send, z_recv, y_send, y_recv, c_send, c_recv, h_send, h_recv,
    n_send, n_recv, p_send, p_recv, o_send, o_recv, q_send, q_recv,
):
    row = lax.axis_index("row")
    col = lax.axis_index("col")
    core = row % NC
    zz = (row // NC) % NZ
    yy = row // (NC * NZ)
    z_dev = [(yy * NZ + (zz + d) % NZ) * NC + core for d in range(NZ)]
    y_dev = [(((yy + d) % NY) * NZ + zz) * NC + core for d in range(NY)]
    mate = row + 1 - 2 * core
    above = (row + 1) % NROW
    below = (row + NROW - 1) % NROW
    x_dev = [(col + d) % NX for d in range(NX)]

    barrier = pltpu.get_barrier_semaphore()
    for dev in z_dev[1:] + y_dev[1:] + [mate, above, below]:
        pl.semaphore_signal(barrier, inc=1, device_id={"row": dev}, device_id_type=MESH)
    for dev in x_dev[1:]:
        pl.semaphore_signal(barrier, inc=1, device_id={"col": dev}, device_id_type=MESH)

    def to_row(src, dst, send, recv, dev):
        return pltpu.make_async_remote_copy(
            src_ref=src, dst_ref=dst, send_sem=send, recv_sem=recv,
            device_id={"row": dev}, device_id_type=MESH,
        )

    def to_col(src, dst, send, recv, dev):
        return pltpu.make_async_remote_copy(
            src_ref=src, dst_ref=dst, send_sem=send, recv_sem=recv,
            device_id={"col": dev}, device_id_type=MESH,
        )

    W[0] = pltpu.roll(res[...], (LANES - col * WIDTH) % LANES, 1)

    def stage_table(k):
        pieces = []
        for c in range(CL_DEV):
            value = dot(cb[c], W[k, pl.ds(c * LEAF_UNKNOWNS, LEAF_UNKNOWNS), :])
            pieces += [value[0:8], value[8:16]]
        T[k, 0, 0, 0] = pack(pieces)

    def stage_halo(k):
        HP[k] = pack([W[k, pl.ds(q * LANES, LANES), :] for q in range(4)])

    stage_table(0)
    stage_halo(0)
    pl.semaphore_wait(barrier, (NZ - 1) + (NY - 1) + 3 + (NX - 1))

    near_out = [
        to_col(near, NB.at[d - 1], n_send.at[d - 1], n_recv.at[d - 1], x_dev[d])
        for d in range(1, NX)
    ]
    coup_out = [
        to_col(coup, CP.at[d - 1], p_send.at[d - 1], p_recv.at[d - 1], x_dev[d])
        for d in range(1, NX)
    ]

    def unpack_table(k, side):
        def one(n, carry):
            value = T[k, side, n // NZ, n % NZ]
            for q in range(4):
                where = side * CL_DEV * NY * NZ + n * CL_DEV + q // 2
                U[where, pl.ds((q % 2) * 8, 8), :] = lanes_to_front(value, q)
            return carry

        lax.fori_loop(0, NY * NZ, one, 0, unroll=8)

    def near_product(k):
        for q in range(4):
            rows = pl.ds((q % 2) * LANES, LANES)
            H[q // 2, rows, :] = lanes_to_front(HB[k, 0], q)
            H[4 + q // 2, rows, :] = lanes_to_front(HB[k, 1], q)
        for c in range(CL_DEV):
            H[2 + c] = W[k, pl.ds(c * LEAF_UNKNOWNS, LEAF_UNKNOWNS), :]
        for c in range(CL_DEV):
            base = CL_DEV * FAR + c * NX
            total = dot(near[c], H[idx[base]])
            for s in range(1, NX):
                total = total + dot(NB[s - 1, c], H[idx[base + s]])
            W[k + 1, pl.ds(c * LEAF_UNKNOWNS, LEAF_UNKNOWNS), :] = total

    def step(k, carry):
        z_out = [
            to_row(T.at[k, 0, 0, 0], T.at[k, 0, 0, d], z_send.at[k], z_recv.at[k], z_dev[d])
            for d in range(1, NZ)
        ]
        z_all = to_row(
            T.at[k, 0, 0, pl.ds(1, NZ - 1)], T.at[k, 0, 0, pl.ds(1, NZ - 1)],
            z_send.at[k], z_recv.at[k], z_dev[1],
        )
        y_out = [
            to_row(T.at[k, 0, 0], T.at[k, 0, d], y_send.at[k, d - 1], y_recv.at[k, d - 1], y_dev[d])
            for d in range(1, NY)
        ]
        c_out = to_row(T.at[k, 0], T.at[k, 1], c_send.at[k], c_recv.at[k], mate)
        halo_out = [
            to_row(HP.at[k], HB.at[k, 0], h_send.at[k, 0], h_recv.at[k, 0], above),
            to_row(HP.at[k], HB.at[k, 1], h_send.at[k, 1], h_recv.at[k, 1], below),
        ]
        for copy in z_out:
            copy.start()
        for copy in halo_out:
            copy.start()

        @pl.when(k == 0)
        def _():
            for copy in coup_out:
                copy.start()
            for copy in near_out:
                copy.start()

        for copy in halo_out:
            copy.wait()

        @pl.when(k > 0)
        def _():
            near_product(k)

        z_all.wait_recv()
        for copy in y_out:
            copy.start()
        for copy in y_out:
            copy.wait_recv()
        c_out.start()
        unpack_table(k, 0)

        @pl.when(k == 0)
        def _():
            for copy in coup_out:
                copy.wait()
            for copy in near_out:
                copy.wait()
            near_product(k)

        c_out.wait()
        for copy in y_out:
            copy.wait_send()
        z_all.wait_send()
        unpack_table(k, 1)

        for c in range(CL_DEV):

            def fetch(p, carry, c=c):
                F[c, pl.ds(p * RANK, RANK), :] = U[idx[c * FAR + p]]
                return carry

            lax.fori_loop(0, FAR, fetch, 0, unroll=8)
        span = SLOTS * RANK
        for c in range(CL_DEV):
            rows = pl.ds(c * RANK, RANK)
            total = dot(coup[rows, :], F[c, pl.ds(0, span), :])
            for s in range(1, NX):
                total = total + dot(CP[s - 1, rows, :], F[c, pl.ds(s * span, span), :])
            W[k + 1, pl.ds(c * LEAF_UNKNOWNS, LEAF_UNKNOWNS), :] += dot(rbt[c], total)

        @pl.when(k < SB - 1)
        def _():
            stage_table(k + 1)
            stage_halo(k + 1)

        return carry

    lax.fori_loop(0, SB, step, 0)

    chunk = 32

    def gather_gram(n, sums):
        vals = [W[a, pl.ds(n * chunk, chunk), :] for a in range(SB + 1)]
        new = []
        for (a, b), old in zip(PAIRS, sums):
            prod = vals[a] * vals[b]
            new.append(old + ((prod[0:8] + prod[8:16]) + (prod[16:24] + prod[24:32])))
        return tuple(new)

    sums = lax.fori_loop(
        0, ROWS // chunk, gather_gram, tuple(jnp.zeros((8, LANES), jnp.float32) for _ in PAIRS)
    )
    GR[...] = jnp.zeros_like(GR)
    for n, value in enumerate(sums):
        GR[pl.ds(n, 1), :] = jnp.sum(value, axis=0, keepdims=True)
    grams = GR[...]
    GZ[0] = pack([grams[0:8], grams[8:16]])
    z_out = [
        to_row(GZ.at[0], GZ.at[d], z_send.at[SB], z_recv.at[SB], z_dev[d]) for d in range(1, NZ)
    ]
    z_all = to_row(
        GZ.at[pl.ds(1, NZ - 1)], GZ.at[pl.ds(1, NZ - 1)], z_send.at[SB], z_recv.at[SB], z_dev[1]
    )
    for copy in z_out:
        copy.start()
    z_all.wait()
    total = GZ[zz % NZ]
    for src in range(1, NZ):
        total = total + GZ[(zz + NZ - src) % NZ]
    GY[0] = total
    y_out = [
        to_row(GY.at[0], GY.at[d], y_send.at[SB, d - 1], y_recv.at[SB, d - 1], y_dev[d])
        for d in range(1, NY)
    ]
    for copy in y_out:
        copy.start()
    for copy in y_out:
        copy.wait()
    total = GY[yy % NY]
    for src in range(1, NY):
        total = total + GY[(yy + NY - src) % NY]
    GC[0] = total
    c_out = to_row(GC.at[0], GC.at[1], c_send.at[SB], c_recv.at[SB], mate)
    c_out.start()
    c_out.wait()
    total = GC[0] + GC[1]
    second = lanes_to_front(total, 1)
    gram = [[None] * (SB + 1) for _ in range(SB + 1)]
    for n, (a, b) in enumerate(PAIRS):
        gram[a][b] = gram[b][a] = total[n : n + 1] if n < 8 else second[n - 8 : n - 7]
    hessen, weights = small_update(gram, 1.0, SB)
    XH[0] = jnp.zeros((24, LANES), jnp.float32)
    for a in range(SB + 1):
        for b in range(SB):
            XH[0, pl.ds(a * SB + b, 1), :] = hessen[a][b]
    pieces = []
    for q in range(4):
        rows = pl.ds(q * LANES, LANES)
        value = weights[0] * W[0, rows, :]
        for k in range(1, SB):
            value = value + weights[k] * W[k, rows, :]
        pieces.append(value)
    XO[0] = pack(pieces)
    last = []
    for d in range(1, NX):
        last.append(to_col(XO.at[0], XO.at[d], o_send.at[d - 1], o_recv.at[d - 1], x_dev[d]))
        last.append(to_col(XH.at[0], XH.at[d], q_send.at[d - 1], q_recv.at[d - 1], x_dev[d]))
    for copy in last:
        copy.start()
    for copy in last:
        copy.wait()
    group = lane_group((LANES, LANES))
    values = [XO[(col + NX - src) % NX] for src in range(NX)]
    for q in range(4):
        rows = pl.ds(q * LANES, LANES)
        value = lanes_to_front(values[0], q)
        for src in range(1, NX):
            shift = ((src - q) * WIDTH) % LANES
            moved = pltpu.roll(values[src], shift, 1) if shift else values[src]
            value = jnp.where(group == src, moved, value)
        out[rows, :] = sol[rows, :] + value
    hout[...] = pack([XH[(col + NX - src) % NX] for src in range(NX)])


def local(
    residual,
    solution,
    near_field_blocks,
    near_cols,
    couplings,
    far_cols,
    far_count,
    col_basis,
    row_basis,
):
    row = lax.axis_index("row")
    col = lax.axis_index("col")
    positions = col * SLOTS + jnp.arange(SLOTS, dtype=jnp.int32)
    live = positions[None, :] < far_count[:, None]
    weighted = jnp.where(live[:, :, None, None], couplings, 0.0)
    weighted = weighted.transpose(0, 2, 1, 3).reshape(CL_DEV * RANK, SLOTS * RANK)
    own = jnp.concatenate([far_cols, near_cols], axis=1)
    lists = [own] + [
        lax.ppermute(own, "col", [(i, (i + s) % NX) for i in range(NX)]) for s in range(1, NX)
    ]
    far = jnp.concatenate([piece[:, :SLOTS] for piece in lists], axis=1)
    near = jnp.concatenate([piece[:, SLOTS:] for piece in lists], axis=1)
    owner = far // CL_DEV
    core, rest = owner % NC, owner // NC
    tile = (
        ((row + NC - core) % NC) * (NY * NZ)
        + ((row // (NC * NZ) + NY - rest // NZ) % NY) * NZ
        + (row // NC + NZ - rest % NZ) % NZ
    )
    idx = jnp.concatenate(
        [
            (tile * CL_DEV + far % CL_DEV).reshape(-1),
            (near - (row * CL_DEV - REACH)).reshape(-1),
        ]
    ).astype(jnp.int32)
    f32 = jnp.float32
    vmem = pl.BlockSpec(memory_space=pltpu.VMEM)
    dma = pltpu.SemaphoreType.DMA
    new_sol, hess = pl.pallas_call(
        kernel,
        out_shape=(
            jax.ShapeDtypeStruct((ROWS, LANES), f32),
            jax.ShapeDtypeStruct((24, LANES), f32),
        ),
        in_specs=[pl.BlockSpec(memory_space=pltpu.SMEM)] + [vmem] * 6,
        out_specs=(vmem, vmem),
        scratch_shapes=[
            pltpu.VMEM((SB + 1, ROWS, LANES), f32),
            pltpu.VMEM((SB, NC, NY, NZ, 8, LANES), f32),
            pltpu.VMEM((NROW * CL_DEV, RANK, LANES), f32),
            pltpu.VMEM((SB, LANES, LANES), f32),
            pltpu.VMEM((SB, 2, LANES, LANES), f32),
            pltpu.VMEM((CL_DEV + 2 * REACH, LEAF_UNKNOWNS, LANES), f32),
            pltpu.VMEM((CL_DEV, FAR * RANK, LANES), f32),
            pltpu.VMEM((NX - 1, CL_DEV, LEAF_UNKNOWNS, LEAF_UNKNOWNS), f32),
            pltpu.VMEM((NX - 1, CL_DEV * RANK, SLOTS * RANK), f32),
            pltpu.VMEM((16, LANES), f32),
            pltpu.VMEM((NZ, 8, LANES), f32),
            pltpu.VMEM((NY, 8, LANES), f32),
            pltpu.VMEM((NC, 8, LANES), f32),
            pltpu.VMEM((NX, LANES, LANES), f32),
            pltpu.VMEM((NX, 24, LANES), f32),
            dma((SB + 1,)), dma((SB + 1,)),
            dma((SB + 1, NY - 1)), dma((SB + 1, NY - 1)),
            dma((SB + 1,)), dma((SB + 1,)),
            dma((SB, 2)), dma((SB, 2)),
            dma((NX - 1,)), dma((NX - 1,)),
            dma((NX - 1,)), dma((NX - 1,)),
            dma((NX - 1,)), dma((NX - 1,)),
            dma((NX - 1,)), dma((NX - 1,)),
        ],
        compiler_params=pltpu.CompilerParams(
            collective_id=0, has_side_effects=True, vmem_limit_bytes=48 * 1024 * 1024
        ),
    )(
        idx,
        residual,
        solution,
        near_field_blocks.reshape(CL_DEV, LEAF_UNKNOWNS, LEAF_UNKNOWNS),
        weighted,
        col_basis,
        row_basis.transpose(0, 2, 1),
    )
    return (new_sol, hess[: (SB + 1) * SB].reshape(SB + 1, SB, LANES))


def solution(mesh):
    placed = (
        P("row", None),
        P("row", None),
        P("row", "col", None, None),
        P("row", "col"),
        P("row", "col", None, None),
        P("row", "col"),
        P("row"),
        P("row", None, None),
        P("row", None, None),
    )
    return jax.shard_map(
        local, mesh=mesh, in_specs=placed, out_specs=(P("row", None), P()), check_vma=False
    )
```

```python
import functools

import jax
import jax.numpy as jnp
from jax import lax
from jax.experimental import pallas as pl
from jax.experimental.pallas import tpu as pltpu
from jax.sharding import PartitionSpec as P

LEAF_UNKNOWNS = 256
CL_DEV = 2
REACH = 2
SB = 4
RANK = 16
LANES = 128
NY, NZ, NC = 4, 16, 2
NX = 4
NROW = NY * NZ * NC
WIDTH = LANES // NX
ROWS = CL_DEV * LEAF_UNKNOWNS
SLOTS = 16
FAR = SLOTS * NX
REACH_Z = NZ // 4
RUNS = [
    run
    for run in ((0, REACH_Z + 1), (NZ - REACH_Z, NZ), (REACH_Z + 1, NZ - REACH_Z))
    if run[1] > run[0]
]
PAIRS = [(a, b) for a in range(SB + 1) for b in range(a, SB + 1)]


HIGH = lax.Precision.HIGHEST
SHIFT = 1.0
MESH = pl.DeviceIdType.MESH


def cholesky_upper(entries, order_n):
    zero_entry = jnp.zeros_like(entries[0][0])
    upper_r = []
    for row_idx in range(order_n):
        upper_r.append([zero_entry] * order_n)
    for row_idx in range(order_n):
        running = entries[row_idx][row_idx]
        for earlier in range(row_idx):
            running = running - upper_r[earlier][row_idx] * upper_r[earlier][row_idx]
        pivot_val = jnp.sqrt(running)
        upper_r[row_idx][row_idx] = pivot_val
        for col_idx in range(row_idx + 1, order_n):
            entry_val = entries[row_idx][col_idx]
            for earlier in range(row_idx):
                entry_val = entry_val - upper_r[earlier][row_idx] * upper_r[earlier][col_idx]
            upper_r[row_idx][col_idx] = entry_val / pivot_val
    return upper_r


def small_update(gram_sum, scale_factor, depth_n):
    order_n = depth_n + 1
    entries = gram_sum
    upper_r = cholesky_upper(entries, order_n)
    shifted = [
        [
            SHIFT * upper_r[row_idx][col_idx] + upper_r[row_idx][col_idx + 1]
            for col_idx in range(depth_n)
        ]
        for row_idx in range(order_n)
    ]
    hessen = []
    for row_idx in range(order_n):
        row_vals = []
        for col_idx in range(depth_n):
            entry_val = shifted[row_idx][col_idx]
            for earlier in range(col_idx):
                entry_val = entry_val - row_vals[earlier] * upper_r[earlier][col_idx]
            row_vals.append(entry_val / upper_r[col_idx][col_idx])
        hessen.append(row_vals)
    normal = []
    for row_idx in range(depth_n):
        row_vals = []
        for col_idx in range(depth_n):
            entry_val = hessen[0][row_idx] * hessen[0][col_idx]
            for inner in range(1, order_n):
                entry_val = entry_val + hessen[inner][row_idx] * hessen[inner][col_idx]
            row_vals.append(entry_val)
        normal.append(row_vals)
    target = [scale_factor * upper_r[0][0] * hessen[0][col_idx] for col_idx in range(depth_n)]
    factor = cholesky_upper(normal, depth_n)
    forward = []
    for row_idx in range(depth_n):
        entry_val = target[row_idx]
        for earlier in range(row_idx):
            entry_val = entry_val - factor[earlier][row_idx] * forward[earlier]
        forward.append(entry_val / factor[row_idx][row_idx])
    solved = [None] * depth_n
    for row_idx in range(depth_n - 1, -1, -1):
        entry_val = forward[row_idx]
        for later in range(row_idx + 1, depth_n):
            entry_val = entry_val - factor[row_idx][later] * solved[later]
        solved[row_idx] = entry_val / factor[row_idx][row_idx]
    weights = [None] * depth_n
    for row_idx in range(depth_n - 1, -1, -1):
        entry_val = solved[row_idx]
        for later in range(row_idx + 1, depth_n):
            entry_val = entry_val - upper_r[row_idx][later] * weights[later]
        weights[row_idx] = entry_val / upper_r[row_idx][row_idx]
    return (hessen, weights)


def dot(left, right):
    return jnp.dot(left, right, precision=HIGH, preferred_element_type=jnp.float32)


def lane_group(shape):
    return lax.broadcasted_iota(jnp.int32, shape, 1) // WIDTH


def pack(pieces):
    group = lane_group(pieces[0].shape)
    out = pieces[0]
    for q in range(1, len(pieces)):
        out = jnp.where(group == q, pltpu.roll(pieces[q], q * WIDTH, 1), out)
    return out


def lanes_to_front(value, q):
    return value if q == 0 else pltpu.roll(value, LANES - q * WIDTH, 1)


def kernel(
    lists, res, sol, near, coup, cb, rbt, out, hout,
    W, T, U, HP, HB, H, F, NB, CP, GR, GZ, GY, GC, XO, XH, IV, IX,
    z_send, z_recv, y_send, y_recv, c_send, c_recv, h_send, h_recv,
    n_send, n_recv, p_send, p_recv, o_send, o_recv, q_send, q_recv,
    i_send, i_recv, i_copy,
):
    row = lax.axis_index("row")
    col = lax.axis_index("col")
    core = row % NC
    zz = (row // NC) % NZ
    yy = row // (NC * NZ)
    z_dev = [(yy * NZ + (zz + d) % NZ) * NC + core for d in range(NZ)]
    y_dev = [(((yy + d) % NY) * NZ + zz) * NC + core for d in range(NY)]
    mate = row + 1 - 2 * core
    above = (row + 1) % NROW
    below = (row + NROW - 1) % NROW
    x_dev = [(col + d) % NX for d in range(NX)]

    barrier = pltpu.get_barrier_semaphore()
    for dev in z_dev[1:] + y_dev[1:] + [mate, above, below]:
        pl.semaphore_signal(barrier, inc=1, device_id={"row": dev}, device_id_type=MESH)
    for dev in x_dev[1:]:
        pl.semaphore_signal(barrier, inc=1, device_id={"col": dev}, device_id_type=MESH)

    def to_row(src, dst, send, recv, dev):
        return pltpu.make_async_remote_copy(
            src_ref=src, dst_ref=dst, send_sem=send, recv_sem=recv,
            device_id={"row": dev}, device_id_type=MESH,
        )

    def to_col(src, dst, send, recv, dev):
        return pltpu.make_async_remote_copy(
            src_ref=src, dst_ref=dst, send_sem=send, recv_sem=recv,
            device_id={"col": dev}, device_id_type=MESH,
        )

    W[0] = pltpu.roll(res[...], (LANES - col * WIDTH) % LANES, 1)

    def stage_table(k):
        pieces = []
        for c in range(CL_DEV):
            value = dot(cb[c], W[k, pl.ds(c * LEAF_UNKNOWNS, LEAF_UNKNOWNS), :])
            pieces += [value[0:8], value[8:16]]
        T[k, 0, 0, 0] = pack(pieces)

    def stage_halo(k):
        HP[k] = pack([W[k, pl.ds(q * LANES, LANES), :] for q in range(4)])

    stage_table(0)
    stage_halo(0)
    pl.semaphore_wait(barrier, (NZ - 1) + (NY - 1) + 3 + (NX - 1))

    right, left = x_dev[1], x_dev[NX - 1]

    def near_copy(n, src, dst, dev):
        return to_col(src, dst, n_send.at[n], n_recv.at[n], dev)

    near_first = [
        near_copy(0, near.at[0], NB.at[0, 0], right),
        near_copy(1, near.at[1], NB.at[2, 1], left),
    ]
    near_second = [
        near_copy(2, near.at[1], NB.at[0, 1], right),
        near_copy(3, near.at[0], NB.at[2, 0], left),
    ]
    near_relay = [
        near_copy(4, NB.at[0, 0], NB.at[1, 0], right),
        near_copy(5, NB.at[2, 1], NB.at[1, 1], left),
    ]
    list_out = [
        to_col(lists, IV.at[d - 1], i_send.at[d - 1], i_recv.at[d - 1], x_dev[d])
        for d in range(1, NX)
    ]
    list_in = [
        pltpu.make_async_copy(lists if d == 0 else IV.at[d - 1], IX.at[d], i_copy.at[d])
        for d in range(NX)
    ]
    coup_out = [
        to_col(coup, CP.at[d - 1], p_send.at[d - 1], p_recv.at[d - 1], x_dev[d])
        for d in range(1, NX)
    ]

    def unpack_table(k, side, run):
        def one(n, carry):
            for y in range(NY):
                value = T[k, side, y, n]
                for q in range(4):
                    where = ((side * NY + y) * NZ + n) * CL_DEV + q // 2
                    U[where, pl.ds((q % 2) * 8, 8), :] = lanes_to_front(value, q)
            return carry

        lax.fori_loop(run[0], run[1], one, 0)

    def near_product(k):
        for q in range(4):
            rows = pl.ds((q % 2) * LANES, LANES)
            H[q // 2, rows, :] = lanes_to_front(HB[k, 0], q)
            H[4 + q // 2, rows, :] = lanes_to_front(HB[k, 1], q)
        for c in range(CL_DEV):
            H[2 + c] = W[k, pl.ds(c * LEAF_UNKNOWNS, LEAF_UNKNOWNS), :]
        for c in range(CL_DEV):
            total = dot(near[c], H[IX[0, c, SLOTS]])
            for s in range(1, NX):
                total = total + dot(NB[s - 1, c], H[IX[s, c, SLOTS]])
            W[k + 1, pl.ds(c * LEAF_UNKNOWNS, LEAF_UNKNOWNS), :] = total

    def step(k, carry):
        z_out = [
            to_row(
                T.at[k, 0, 0, 0], T.at[k, 0, 0, d], z_send.at[k],
                z_recv.at[k, [d >= lo and d < hi for lo, hi in RUNS].index(True)], z_dev[d],
            )
            for d in sorted(range(1, NZ), key=lambda d: -min(d, NZ - d))
        ]
        z_all = to_row(
            T.at[k, 0, 0, pl.ds(1, NZ - 1)], T.at[k, 0, 0, pl.ds(1, NZ - 1)],
            z_send.at[k], z_recv.at[k, 0], z_dev[1],
        )
        z_in, y_out, c_out = [], [], []
        for n, (lo, hi) in enumerate(RUNS):
            got = pl.ds(max(lo, 1), hi - max(lo, 1))
            z_in.append(
                to_row(T.at[k, 0, 0, got], T.at[k, 0, 0, got], z_send.at[k], z_recv.at[k, n], z_dev[1])
                if hi > 1 else None
            )
            run = pl.ds(lo, hi - lo)
            y_out.append([
                to_row(
                    T.at[k, 0, 0, run], T.at[k, 0, d, run],
                    y_send.at[k, n, d - 1], y_recv.at[k, n, d - 1], y_dev[d],
                )
                for d in range(1, NY)
            ])
            c_out.append(
                to_row(
                    T.at[k, 0, :, run], T.at[k, 1, :, run], c_send.at[k, n], c_recv.at[k, n], mate
                )
            )
        halo_out = [
            to_row(HP.at[k], HB.at[k, 0], h_send.at[k, 0], h_recv.at[k, 0], above),
            to_row(HP.at[k], HB.at[k, 1], h_send.at[k, 1], h_recv.at[k, 1], below),
        ]
        for copy in z_out:
            copy.start()
        for copy in halo_out:
            copy.start()

        @pl.when(k == 0)
        def _():
            for copy in list_out + coup_out + near_first + near_second:
                copy.start()

        for copy in halo_out:
            copy.wait()

        @pl.when(k > 0)
        def _():
            near_product(k)

        for n in range(len(RUNS)):
            if z_in[n] is not None:
                z_in[n].wait_recv()
            for copy in y_out[n]:
                copy.start()

        @pl.when(k == 0)
        def _():
            for copy, relay in zip(near_first, near_relay):
                copy.wait_recv()
                relay.start()
            for copy in list_out:
                copy.wait()
            for copy in list_in:
                copy.start()

        for n, run in enumerate(RUNS):
            for copy in y_out[n]:
                copy.wait_recv()
            c_out[n].start()
            unpack_table(k, 0, run)

        @pl.when(k == 0)
        def _():
            for copy in list_in:
                copy.wait()
            for copy in coup_out:
                copy.wait()
            for copy in near_first:
                copy.wait_send()
            for copy in near_second + near_relay:
                copy.wait()
            near_product(k)

        for n, run in enumerate(RUNS):
            c_out[n].wait_recv()
            unpack_table(k, 1, run)
        z_all.wait_send()
        for n in range(len(RUNS)):
            for copy in y_out[n]:
                copy.wait_send()
            c_out[n].wait_send()

        for c in range(CL_DEV):
            for s in range(NX):

                def fetch(p, carry, c=c, s=s):
                    F[c, pl.ds((s * SLOTS + p) * RANK, RANK), :] = U[IX[s, c, p]]
                    return carry

                lax.fori_loop(0, SLOTS, fetch, 0, unroll=8)
        span = SLOTS * RANK
        for c in range(CL_DEV):
            rows = pl.ds(c * RANK, RANK)
            total = dot(coup[rows, :], F[c, pl.ds(0, span), :])
            for s in range(1, NX):
                total = total + dot(CP[s - 1, rows, :], F[c, pl.ds(s * span, span), :])
            W[k + 1, pl.ds(c * LEAF_UNKNOWNS, LEAF_UNKNOWNS), :] += dot(rbt[c], total)

        @pl.when(k < SB - 1)
        def _():
            stage_table(k + 1)
            stage_halo(k + 1)

        return carry

    lax.fori_loop(0, SB, step, 0)

    chunk = 32

    def gather_gram(n, sums):
        vals = [W[a, pl.ds(n * chunk, chunk), :] for a in range(SB + 1)]
        new = []
        for (a, b), old in zip(PAIRS, sums):
            prod = vals[a] * vals[b]
            new.append(old + ((prod[0:8] + prod[8:16]) + (prod[16:24] + prod[24:32])))
        return tuple(new)

    sums = lax.fori_loop(
        0, ROWS // chunk, gather_gram, tuple(jnp.zeros((8, LANES), jnp.float32) for _ in PAIRS)
    )
    GR[...] = jnp.zeros_like(GR)
    for n, value in enumerate(sums):
        GR[pl.ds(n, 1), :] = jnp.sum(value, axis=0, keepdims=True)
    grams = GR[...]
    GZ[0] = pack([grams[0:8], grams[8:16]])
    z_out = [
        to_row(GZ.at[0], GZ.at[d], z_send.at[SB], z_recv.at[SB, 0], z_dev[d]) for d in range(1, NZ)
    ]
    z_all = to_row(
        GZ.at[pl.ds(1, NZ - 1)], GZ.at[pl.ds(1, NZ - 1)], z_send.at[SB], z_recv.at[SB, 0], z_dev[1]
    )
    for copy in z_out:
        copy.start()
    z_all.wait()
    total = GZ[zz % NZ]
    for src in range(1, NZ):
        total = total + GZ[(zz + NZ - src) % NZ]
    GY[0] = total
    y_out = [
        to_row(GY.at[0], GY.at[d], y_send.at[SB, 0, d - 1], y_recv.at[SB, 0, d - 1], y_dev[d])
        for d in range(1, NY)
    ]
    for copy in y_out:
        copy.start()
    for copy in y_out:
        copy.wait()
    total = GY[yy % NY]
    for src in range(1, NY):
        total = total + GY[(yy + NY - src) % NY]
    GC[0] = total
    c_out = to_row(GC.at[0], GC.at[1], c_send.at[SB, 0], c_recv.at[SB, 0], mate)
    c_out.start()
    c_out.wait()
    total = GC[0] + GC[1]
    second = lanes_to_front(total, 1)
    gram = [[None] * (SB + 1) for _ in range(SB + 1)]
    for n, (a, b) in enumerate(PAIRS):
        gram[a][b] = gram[b][a] = total[n : n + 1] if n < 8 else second[n - 8 : n - 7]
    hessen, weights = small_update(gram, 1.0, SB)
    XH[0] = jnp.zeros((24, LANES), jnp.float32)
    for a in range(SB + 1):
        for b in range(SB):
            XH[0, pl.ds(a * SB + b, 1), :] = hessen[a][b]
    pieces = []
    for q in range(4):
        rows = pl.ds(q * LANES, LANES)
        value = weights[0] * W[0, rows, :]
        for k in range(1, SB):
            value = value + weights[k] * W[k, rows, :]
        pieces.append(value)
    XO[0] = pack(pieces)
    last = []
    for d in range(1, NX):
        last.append(to_col(XO.at[0], XO.at[d], o_send.at[d - 1], o_recv.at[d - 1], x_dev[d]))
        last.append(to_col(XH.at[0], XH.at[d], q_send.at[d - 1], q_recv.at[d - 1], x_dev[d]))
    for copy in last:
        copy.start()
    for copy in last:
        copy.wait()
    group = lane_group((LANES, LANES))
    values = [XO[(col + NX - src) % NX] for src in range(NX)]
    for q in range(4):
        rows = pl.ds(q * LANES, LANES)
        value = lanes_to_front(values[0], q)
        for src in range(1, NX):
            shift = ((src - q) * WIDTH) % LANES
            moved = pltpu.roll(values[src], shift, 1) if shift else values[src]
            value = jnp.where(group == src, moved, value)
        out[rows, :] = sol[rows, :] + value
    hout[...] = pack([XH[(col + NX - src) % NX] for src in range(NX)])


def local(
    residual,
    solution,
    near_field_blocks,
    near_cols,
    couplings,
    far_cols,
    far_count,
    col_basis,
    row_basis,
):
    row = lax.axis_index("row")
    col = lax.axis_index("col")
    positions = col * SLOTS + jnp.arange(SLOTS, dtype=jnp.int32)
    live = positions[None, :] < far_count[:, None]
    weighted = jnp.where(live[:, :, None, None], couplings, 0.0)
    weighted = weighted.transpose(0, 2, 1, 3).reshape(CL_DEV * RANK, SLOTS * RANK)
    owner = far_cols // CL_DEV
    core, rest = owner % NC, owner // NC
    tile = (
        ((row + NC - core) % NC) * (NY * NZ)
        + ((row // (NC * NZ) + NY - rest // NZ) % NY) * NZ
        + (row // NC + NZ - rest % NZ) % NZ
    )
    lists = jnp.concatenate(
        [tile * CL_DEV + far_cols % CL_DEV, near_cols - (row * CL_DEV - REACH)], axis=1
    ).astype(jnp.int32)
    lists = jnp.pad(lists, ((0, 8 - CL_DEV), (0, LANES - SLOTS - 1)))
    f32 = jnp.float32
    vmem = pl.BlockSpec(memory_space=pltpu.VMEM)
    dma = pltpu.SemaphoreType.DMA
    new_sol, hess = pl.pallas_call(
        kernel,
        out_shape=(
            jax.ShapeDtypeStruct((ROWS, LANES), f32),
            jax.ShapeDtypeStruct((24, LANES), f32),
        ),
        in_specs=[vmem] * 7,
        out_specs=(vmem, vmem),
        scratch_shapes=[
            pltpu.VMEM((SB + 1, ROWS, LANES), f32),
            pltpu.VMEM((SB, NC, NY, NZ, 8, LANES), f32),
            pltpu.VMEM((NROW * CL_DEV, RANK, LANES), f32),
            pltpu.VMEM((SB, LANES, LANES), f32),
            pltpu.VMEM((SB, 2, LANES, LANES), f32),
            pltpu.VMEM((CL_DEV + 2 * REACH, LEAF_UNKNOWNS, LANES), f32),
            pltpu.VMEM((CL_DEV, FAR * RANK, LANES), f32),
            pltpu.VMEM((NX - 1, CL_DEV, LEAF_UNKNOWNS, LEAF_UNKNOWNS), f32),
            pltpu.VMEM((NX - 1, CL_DEV * RANK, SLOTS * RANK), f32),
            pltpu.VMEM((16, LANES), f32),
            pltpu.VMEM((NZ, 8, LANES), f32),
            pltpu.VMEM((NY, 8, LANES), f32),
            pltpu.VMEM((NC, 8, LANES), f32),
            pltpu.VMEM((NX, LANES, LANES), f32),
            pltpu.VMEM((NX, 24, LANES), f32),
            pltpu.VMEM((NX - 1, 8, LANES), jnp.int32),
            pltpu.SMEM((NX, 8, LANES), jnp.int32),
            dma((SB + 1,)), dma((SB + 1, len(RUNS))),
            dma((SB + 1, len(RUNS), NY - 1)), dma((SB + 1, len(RUNS), NY - 1)),
            dma((SB + 1, len(RUNS))), dma((SB + 1, len(RUNS))),
            dma((SB, 2)), dma((SB, 2)),
            dma((6,)), dma((6,)),
            dma((NX - 1,)), dma((NX - 1,)),
            dma((NX - 1,)), dma((NX - 1,)),
            dma((NX - 1,)), dma((NX - 1,)),
            dma((NX - 1,)), dma((NX - 1,)), dma((NX,)),
        ],
        compiler_params=pltpu.CompilerParams(
            collective_id=0, has_side_effects=True, vmem_limit_bytes=48 * 1024 * 1024
        ),
    )(
        lists,
        residual,
        solution,
        near_field_blocks.reshape(CL_DEV, LEAF_UNKNOWNS, LEAF_UNKNOWNS),
        weighted,
        col_basis,
        row_basis.transpose(0, 2, 1),
    )
    return (new_sol, hess[: (SB + 1) * SB].reshape(SB + 1, SB, LANES))


def solution(mesh):
    placed = (
        P("row", None),
        P("row", None),
        P("row", "col", None, None),
        P("row", "col"),
        P("row", "col", None, None),
        P("row", "col"),
        P("row"),
        P("row", None, None),
        P("row", None, None),
    )
    return jax.shard_map(
        local, mesh=mesh, in_specs=placed, out_specs=(P("row", None), P()), check_vma=False
    )
```

```python
import functools

import jax
import jax.numpy as jnp
from jax import lax
from jax.experimental import pallas as pl
from jax.experimental.pallas import tpu as pltpu
from jax.sharding import PartitionSpec as P

LEAF_UNKNOWNS = 256
CL_DEV = 2
REACH = 2
SB = 4
RANK = 16
LANES = 128
NY, NZ, NC = 4, 16, 2
NX = 4
NROW = NY * NZ * NC
WIDTH = LANES // NX
ROWS = CL_DEV * LEAF_UNKNOWNS
SLOTS = 16
FAR = SLOTS * NX
REACH_Z = NZ // 4
RUNS = [
    run
    for run in ((0, REACH_Z + 1), (NZ - REACH_Z, NZ), (REACH_Z + 1, NZ - REACH_Z))
    if run[1] > run[0]
]
PAIRS = [(a, b) for a in range(SB + 1) for b in range(a, SB + 1)]


HIGH = lax.Precision.HIGH
SHIFT = 1.0
MESH = pl.DeviceIdType.MESH


def cholesky_upper(entries, order_n):
    zero_entry = jnp.zeros_like(entries[0][0])
    upper_r = []
    for row_idx in range(order_n):
        upper_r.append([zero_entry] * order_n)
    for row_idx in range(order_n):
        running = entries[row_idx][row_idx]
        for earlier in range(row_idx):
            running = running - upper_r[earlier][row_idx] * upper_r[earlier][row_idx]
        pivot_val = jnp.sqrt(running)
        upper_r[row_idx][row_idx] = pivot_val
        for col_idx in range(row_idx + 1, order_n):
            entry_val = entries[row_idx][col_idx]
            for earlier in range(row_idx):
                entry_val = entry_val - upper_r[earlier][row_idx] * upper_r[earlier][col_idx]
            upper_r[row_idx][col_idx] = entry_val / pivot_val
    return upper_r


def small_update(gram_sum, scale_factor, depth_n):
    order_n = depth_n + 1
    entries = gram_sum
    upper_r = cholesky_upper(entries, order_n)
    shifted = [
        [
            SHIFT * upper_r[row_idx][col_idx] + upper_r[row_idx][col_idx + 1]
            for col_idx in range(depth_n)
        ]
        for row_idx in range(order_n)
    ]
    hessen = []
    for row_idx in range(order_n):
        row_vals = []
        for col_idx in range(depth_n):
            entry_val = shifted[row_idx][col_idx]
            for earlier in range(col_idx):
                entry_val = entry_val - row_vals[earlier] * upper_r[earlier][col_idx]
            row_vals.append(entry_val / upper_r[col_idx][col_idx])
        hessen.append(row_vals)
    normal = []
    for row_idx in range(depth_n):
        row_vals = []
        for col_idx in range(depth_n):
            entry_val = hessen[0][row_idx] * hessen[0][col_idx]
            for inner in range(1, order_n):
                entry_val = entry_val + hessen[inner][row_idx] * hessen[inner][col_idx]
            row_vals.append(entry_val)
        normal.append(row_vals)
    target = [scale_factor * upper_r[0][0] * hessen[0][col_idx] for col_idx in range(depth_n)]
    factor = cholesky_upper(normal, depth_n)
    forward = []
    for row_idx in range(depth_n):
        entry_val = target[row_idx]
        for earlier in range(row_idx):
            entry_val = entry_val - factor[earlier][row_idx] * forward[earlier]
        forward.append(entry_val / factor[row_idx][row_idx])
    solved = [None] * depth_n
    for row_idx in range(depth_n - 1, -1, -1):
        entry_val = forward[row_idx]
        for later in range(row_idx + 1, depth_n):
            entry_val = entry_val - factor[row_idx][later] * solved[later]
        solved[row_idx] = entry_val / factor[row_idx][row_idx]
    weights = [None] * depth_n
    for row_idx in range(depth_n - 1, -1, -1):
        entry_val = solved[row_idx]
        for later in range(row_idx + 1, depth_n):
            entry_val = entry_val - upper_r[row_idx][later] * weights[later]
        weights[row_idx] = entry_val / upper_r[row_idx][row_idx]
    return (hessen, weights)


def dot(left, right):
    return jnp.dot(left, right, precision=HIGH, preferred_element_type=jnp.float32)


def lane_group(shape):
    return lax.broadcasted_iota(jnp.int32, shape, 1) // WIDTH


def pack(pieces):
    group = lane_group(pieces[0].shape)
    out = pieces[0]
    for q in range(1, len(pieces)):
        out = jnp.where(group == q, pltpu.roll(pieces[q], q * WIDTH, 1), out)
    return out


def lanes_to_front(value, q):
    return value if q == 0 else pltpu.roll(value, LANES - q * WIDTH, 1)


def kernel(
    lists, res, sol, near, coup, cb, rbt, out, hout,
    W, T, U, HP, HB, H, F, NB, CP, GR, GZ, GY, GC, WF, XH, IV, IX,
    z_send, z_recv, y_send, y_recv, c_send, c_recv, h_send, h_recv,
    n_send, n_recv, p_send, p_recv, o_send, o_recv, q_send, q_recv,
    i_send, i_recv, i_copy,
):
    row = lax.axis_index("row")
    col = lax.axis_index("col")
    core = row % NC
    zz = (row // NC) % NZ
    yy = row // (NC * NZ)
    z_dev = [(yy * NZ + (zz + d) % NZ) * NC + core for d in range(NZ)]
    y_dev = [(((yy + d) % NY) * NZ + zz) * NC + core for d in range(NY)]
    mate = row + 1 - 2 * core
    above = (row + 1) % NROW
    below = (row + NROW - 1) % NROW
    x_dev = [(col + d) % NX for d in range(NX)]

    barrier = pltpu.get_barrier_semaphore()
    for dev in z_dev[1:] + y_dev[1:] + [mate, above, below]:
        pl.semaphore_signal(barrier, inc=1, device_id={"row": dev}, device_id_type=MESH)
    for dev in x_dev[1:]:
        pl.semaphore_signal(barrier, inc=1, device_id={"col": dev}, device_id_type=MESH)

    def to_row(src, dst, send, recv, dev):
        return pltpu.make_async_remote_copy(
            src_ref=src, dst_ref=dst, send_sem=send, recv_sem=recv,
            device_id={"row": dev}, device_id_type=MESH,
        )

    def to_col(src, dst, send, recv, dev):
        return pltpu.make_async_remote_copy(
            src_ref=src, dst_ref=dst, send_sem=send, recv_sem=recv,
            device_id={"col": dev}, device_id_type=MESH,
        )

    W[0] = pltpu.roll(res[...], (LANES - col * WIDTH) % LANES, 1)

    def stage_table(k):
        pieces = []
        for c in range(CL_DEV):
            value = dot(cb[c], W[k, pl.ds(c * LEAF_UNKNOWNS, LEAF_UNKNOWNS), :])
            pieces += [value[0:8], value[8:16]]
        T[k, 0, 0, 0] = pack(pieces)

    def stage_halo(k):
        HP[k, 0] = pack([W[k, pl.ds(q * LANES, LANES), :] for q in range(4)])

    stage_table(0)
    stage_halo(0)
    pl.semaphore_wait(barrier, (NZ - 1) + (NY - 1) + 3 + (NX - 1))

    right, left = x_dev[1], x_dev[NX - 1]

    def near_copy(n, src, dst, dev):
        return to_col(src, dst, n_send.at[n], n_recv.at[n], dev)

    near_first = [
        near_copy(0, near.at[0], NB.at[0, 0], right),
        near_copy(1, near.at[1], NB.at[2, 1], left),
    ]
    near_second = [
        near_copy(2, near.at[1], NB.at[0, 1], right),
        near_copy(3, near.at[0], NB.at[2, 0], left),
    ]
    near_relay = [
        near_copy(4, NB.at[0, 0], NB.at[1, 0], right),
        near_copy(5, NB.at[2, 1], NB.at[1, 1], left),
    ]
    list_out = [
        to_col(lists, IV.at[d - 1], i_send.at[d - 1], i_recv.at[d - 1], x_dev[d])
        for d in range(1, NX)
    ]
    list_in = [
        pltpu.make_async_copy(lists if d == 0 else IV.at[d - 1], IX.at[d], i_copy.at[d])
        for d in range(NX)
    ]
    coup_out = [
        to_col(coup, CP.at[d - 1], p_send.at[d - 1], p_recv.at[d - 1], x_dev[d])
        for d in range(1, NX)
    ]

    def unpack_table(k, side, run):
        def one(n, carry):
            for y in range(NY):
                value = T[k, side, y, n]
                for q in range(4):
                    where = ((side * NY + y) * NZ + n) * CL_DEV + q // 2
                    U[where, pl.ds((q % 2) * 8, 8), :] = lanes_to_front(value, q)
            return carry

        lax.fori_loop(run[0], run[1], one, 0)

    def panel_copies(k):
        return [
            to_col(
                HP.at[k, 0], HP.at[k, d], o_send.at[k - 1, d - 1], o_recv.at[k - 1, d - 1], x_dev[d]
            )
            for d in range(1, NX)
        ]

    def near_product(k):
        for q in range(4):
            rows = pl.ds((q % 2) * LANES, LANES)
            H[q // 2, rows, :] = lanes_to_front(HB[k, 0], q)
            H[4 + q // 2, rows, :] = lanes_to_front(HB[k, 1], q)
        for c in range(CL_DEV):
            H[2 + c] = W[k, pl.ds(c * LEAF_UNKNOWNS, LEAF_UNKNOWNS), :]
        for c in range(CL_DEV):
            total = dot(near[c], H[IX[0, c, SLOTS]])
            for s in range(1, NX):
                total = total + dot(NB[s - 1, c], H[IX[s, c, SLOTS]])
            W[k + 1, pl.ds(c * LEAF_UNKNOWNS, LEAF_UNKNOWNS), :] = total

    def step(k, carry):
        z_out = [
            to_row(
                T.at[k, 0, 0, 0], T.at[k, 0, 0, d], z_send.at[k],
                z_recv.at[k, [d >= lo and d < hi for lo, hi in RUNS].index(True)], z_dev[d],
            )
            for d in sorted(range(1, NZ), key=lambda d: -min(d, NZ - d))
        ]
        z_all = to_row(
            T.at[k, 0, 0, pl.ds(1, NZ - 1)], T.at[k, 0, 0, pl.ds(1, NZ - 1)],
            z_send.at[k], z_recv.at[k, 0], z_dev[1],
        )
        z_in, y_out, c_out = [], [], []
        for n, (lo, hi) in enumerate(RUNS):
            got = pl.ds(max(lo, 1), hi - max(lo, 1))
            z_in.append(
                to_row(T.at[k, 0, 0, got], T.at[k, 0, 0, got], z_send.at[k], z_recv.at[k, n], z_dev[1])
                if hi > 1 else None
            )
            run = pl.ds(lo, hi - lo)
            y_out.append([
                to_row(
                    T.at[k, 0, 0, run], T.at[k, 0, d, run],
                    y_send.at[k, n, d - 1], y_recv.at[k, n, d - 1], y_dev[d],
                )
                for d in range(1, NY)
            ])
            c_out.append(
                to_row(
                    T.at[k, 0, :, run], T.at[k, 1, :, run], c_send.at[k, n], c_recv.at[k, n], mate
                )
            )
        halo_out = [
            to_row(HP.at[k, 0], HB.at[k, 0], h_send.at[k, 0], h_recv.at[k, 0], above),
            to_row(HP.at[k, 0], HB.at[k, 1], h_send.at[k, 1], h_recv.at[k, 1], below),
        ]
        for copy in z_out:
            copy.start()
        for copy in halo_out:
            copy.start()

        @pl.when(k == 0)
        def _():
            for copy in list_out + coup_out + near_first + near_second:
                copy.start()

        for copy in halo_out:
            copy.wait()

        @pl.when(k > 0)
        def _():
            for copy in panel_copies(k):
                copy.start()

        for n in range(len(RUNS)):
            if n == len(RUNS) - 1:

                @pl.when(k > 0)
                def _():
                    near_product(k)

            if z_in[n] is not None:
                z_in[n].wait_recv()
            for copy in y_out[n]:
                copy.start()

        @pl.when(k == 0)
        def _():
            for copy, relay in zip(near_first, near_relay):
                copy.wait_recv()
                relay.start()
            for copy in list_out:
                copy.wait()
            for copy in list_in:
                copy.start()

        for n, run in enumerate(RUNS):
            for copy in y_out[n]:
                copy.wait_recv()
            c_out[n].start()
            unpack_table(k, 0, run)

        @pl.when(k == 0)
        def _():
            for copy in list_in:
                copy.wait()
            for copy in coup_out:
                copy.wait()
            for copy in near_first:
                copy.wait_send()
            for copy in near_second + near_relay:
                copy.wait()
            near_product(k)

        for n, run in enumerate(RUNS):
            c_out[n].wait_recv()
            unpack_table(k, 1, run)
        z_all.wait_send()
        for n in range(len(RUNS)):
            for copy in y_out[n]:
                copy.wait_send()
            c_out[n].wait_send()

        for c in range(CL_DEV):
            for s in range(NX):

                def fetch(p, carry, c=c, s=s):
                    F[c, pl.ds((s * SLOTS + p) * RANK, RANK), :] = U[IX[s, c, p]]
                    return carry

                lax.fori_loop(0, SLOTS, fetch, 0, unroll=8)
        span = SLOTS * RANK
        for c in range(CL_DEV):
            rows = pl.ds(c * RANK, RANK)
            total = dot(coup[rows, :], F[c, pl.ds(0, span), :])
            for s in range(1, NX):
                total = total + dot(CP[s - 1, rows, :], F[c, pl.ds(s * span, span), :])
            W[k + 1, pl.ds(c * LEAF_UNKNOWNS, LEAF_UNKNOWNS), :] += dot(rbt[c], total)

        @pl.when(k < SB - 1)
        def _():
            stage_table(k + 1)
            stage_halo(k + 1)

        return carry

    lax.fori_loop(0, SB, step, 0)

    chunk = 32

    def gather_gram(n, sums):
        vals = [W[a, pl.ds(n * chunk, chunk), :] for a in range(SB + 1)]
        new = []
        for (a, b), old in zip(PAIRS, sums):
            prod = vals[a] * vals[b]
            new.append(old + ((prod[0:8] + prod[8:16]) + (prod[16:24] + prod[24:32])))
        return tuple(new)

    sums = lax.fori_loop(
        0, ROWS // chunk, gather_gram, tuple(jnp.zeros((8, LANES), jnp.float32) for _ in PAIRS)
    )
    GR[...] = jnp.zeros_like(GR)
    for n, value in enumerate(sums):
        GR[pl.ds(n, 1), :] = jnp.sum(value, axis=0, keepdims=True)
    grams = GR[...]
    GZ[0] = pack([grams[0:8], grams[8:16]])
    z_out = [
        to_row(GZ.at[0], GZ.at[d], z_send.at[SB], z_recv.at[SB, 0], z_dev[d]) for d in range(1, NZ)
    ]
    z_all = to_row(
        GZ.at[pl.ds(1, NZ - 1)], GZ.at[pl.ds(1, NZ - 1)], z_send.at[SB], z_recv.at[SB, 0], z_dev[1]
    )
    for copy in z_out:
        copy.start()
    group = lane_group((LANES, LANES))
    for k in range(1, SB):
        for copy in panel_copies(k):
            copy.wait()
        for q in range(4):
            full = lanes_to_front(HP[k, col % NX], q)
            for src in range(1, NX):
                moved = HP[k, (col + NX - src) % NX]
                if src != q:
                    moved = pltpu.roll(moved, ((src - q) * WIDTH) % LANES, 1)
                full = jnp.where(group == src, moved, full)
            WF[k - 1, pl.ds(q * LANES, LANES), :] = full
    z_all.wait()
    total = GZ[zz % NZ]
    for src in range(1, NZ):
        total = total + GZ[(zz + NZ - src) % NZ]
    GY[0] = total
    y_out = [
        to_row(GY.at[0], GY.at[d], y_send.at[SB, 0, d - 1], y_recv.at[SB, 0, d - 1], y_dev[d])
        for d in range(1, NY)
    ]
    for copy in y_out:
        copy.start()
    for copy in y_out:
        copy.wait()
    total = GY[yy % NY]
    for src in range(1, NY):
        total = total + GY[(yy + NY - src) % NY]
    GC[0] = total
    c_out = to_row(GC.at[0], GC.at[1], c_send.at[SB, 0], c_recv.at[SB, 0], mate)
    c_out.start()
    c_out.wait()
    total = GC[0] + GC[1]
    second = lanes_to_front(total, 1)
    gram = [[None] * (SB + 1) for _ in range(SB + 1)]
    for n, (a, b) in enumerate(PAIRS):
        gram[a][b] = gram[b][a] = total[n : n + 1] if n < 8 else second[n - 8 : n - 7]
    hessen, weights = small_update(gram, 1.0, SB)
    for a in range(SB + 1):
        for b in range(SB):
            XH[0, pl.ds(a * SB + b, 1), :] = hessen[a][b]
    for k in range(SB):
        XH[0, pl.ds((SB + 1) * SB + k, 1), :] = weights[k]
    last = [
        to_col(XH.at[0], XH.at[d], q_send.at[d - 1], q_recv.at[d - 1], x_dev[d])
        for d in range(1, NX)
    ]
    for copy in last:
        copy.start()
    for copy in last:
        copy.wait()
    both = pack([XH[(col + NX - src) % NX] for src in range(NX)])
    hout[...] = both
    full = [both[(SB + 1) * SB + k : (SB + 1) * SB + k + 1] for k in range(SB)]
    for q in range(4):
        rows = pl.ds(q * LANES, LANES)
        value = sol[rows, :] + full[0] * res[rows, :]
        for k in range(1, SB):
            value = value + full[k] * WF[k - 1, rows, :]
        out[rows, :] = value


def local(
    residual,
    solution,
    near_field_blocks,
    near_cols,
    couplings,
    far_cols,
    far_count,
    col_basis,
    row_basis,
):
    row = lax.axis_index("row")
    col = lax.axis_index("col")
    positions = col * SLOTS + jnp.arange(SLOTS, dtype=jnp.int32)
    live = positions[None, :] < far_count[:, None]
    weighted = jnp.where(live[:, :, None, None], couplings, 0.0)
    weighted = weighted.transpose(0, 2, 1, 3).reshape(CL_DEV * RANK, SLOTS * RANK)
    owner = far_cols // CL_DEV
    core, rest = owner % NC, owner // NC
    tile = (
        ((row + NC - core) % NC) * (NY * NZ)
        + ((row // (NC * NZ) + NY - rest // NZ) % NY) * NZ
        + (row // NC + NZ - rest % NZ) % NZ
    )
    lists = jnp.concatenate(
        [tile * CL_DEV + far_cols % CL_DEV, near_cols - (row * CL_DEV - REACH)], axis=1
    ).astype(jnp.int32)
    lists = jnp.pad(lists, ((0, 8 - CL_DEV), (0, LANES - SLOTS - 1)))
    f32 = jnp.float32
    vmem = pl.BlockSpec(memory_space=pltpu.VMEM)
    dma = pltpu.SemaphoreType.DMA
    new_sol, hess = pl.pallas_call(
        kernel,
        out_shape=(
            jax.ShapeDtypeStruct((ROWS, LANES), f32),
            jax.ShapeDtypeStruct((24, LANES), f32),
        ),
        in_specs=[vmem] * 7,
        out_specs=(vmem, vmem),
        scratch_shapes=[
            pltpu.VMEM((SB + 1, ROWS, LANES), f32),
            pltpu.VMEM((SB, NC, NY, NZ, 8, LANES), f32),
            pltpu.VMEM((NROW * CL_DEV, RANK, LANES), f32),
            pltpu.VMEM((SB, NX, LANES, LANES), f32),
            pltpu.VMEM((SB, 2, LANES, LANES), f32),
            pltpu.VMEM((CL_DEV + 2 * REACH, LEAF_UNKNOWNS, LANES), f32),
            pltpu.VMEM((CL_DEV, FAR * RANK, LANES), f32),
            pltpu.VMEM((NX - 1, CL_DEV, LEAF_UNKNOWNS, LEAF_UNKNOWNS), f32),
            pltpu.VMEM((NX - 1, CL_DEV * RANK, SLOTS * RANK), f32),
            pltpu.VMEM((16, LANES), f32),
            pltpu.VMEM((NZ, 8, LANES), f32),
            pltpu.VMEM((NY, 8, LANES), f32),
            pltpu.VMEM((NC, 8, LANES), f32),
            pltpu.VMEM((SB - 1, ROWS, LANES), f32),
            pltpu.VMEM((NX, 24, LANES), f32),
            pltpu.VMEM((NX - 1, 8, LANES), jnp.int32),
            pltpu.SMEM((NX, 8, LANES), jnp.int32),
            dma((SB + 1,)), dma((SB + 1, len(RUNS))),
            dma((SB + 1, len(RUNS), NY - 1)), dma((SB + 1, len(RUNS), NY - 1)),
            dma((SB + 1, len(RUNS))), dma((SB + 1, len(RUNS))),
            dma((SB, 2)), dma((SB, 2)),
            dma((6,)), dma((6,)),
            dma((NX - 1,)), dma((NX - 1,)),
            dma((SB - 1, NX - 1)), dma((SB - 1, NX - 1)),
            dma((NX - 1,)), dma((NX - 1,)),
            dma((NX - 1,)), dma((NX - 1,)), dma((NX,)),
        ],
        compiler_params=pltpu.CompilerParams(
            collective_id=0, has_side_effects=True, vmem_limit_bytes=48 * 1024 * 1024
        ),
    )(
        lists,
        residual,
        solution,
        near_field_blocks.reshape(CL_DEV, LEAF_UNKNOWNS, LEAF_UNKNOWNS),
        weighted,
        col_basis,
        row_basis.transpose(0, 2, 1),
    )
    return (new_sol, hess[: (SB + 1) * SB].reshape(SB + 1, SB, LANES))


def solution(mesh):
    placed = (
        P("row", None),
        P("row", None),
        P("row", "col", None, None),
        P("row", "col"),
        P("row", "col", None, None),
        P("row", "col"),
        P("row"),
        P("row", None, None),
        P("row", None, None),
    )
    return jax.shard_map(
        local, mesh=mesh, in_specs=placed, out_specs=(P("row", None), P()), check_vma=False
    )
```

```python
import functools

import jax
import jax.numpy as jnp
from jax import lax
from jax.experimental import pallas as pl
from jax.experimental.pallas import tpu as pltpu
from jax.sharding import PartitionSpec as P

LEAF_UNKNOWNS = 256
CL_DEV = 2
REACH = 2
SB = 4
RANK = 16
LANES = 128
NY, NZ, NC = 4, 16, 2
NX = 4
NROW = NY * NZ * NC
WIDTH = LANES // NX
ROWS = CL_DEV * LEAF_UNKNOWNS
SLOTS = 16
FAR = SLOTS * NX
REACH_Z = NZ // 4
RUNS = [
    run
    for run in ((0, REACH_Z + 1), (NZ - REACH_Z, NZ), (REACH_Z + 1, NZ - REACH_Z))
    if run[1] > run[0]
]
PAIRS = [(a, b) for a in range(SB + 1) for b in range(a, SB + 1)]


HIGH = lax.Precision.HIGH
SHIFT = 1.0
MESH = pl.DeviceIdType.MESH


def cholesky_upper(entries, order_n):
    zero_entry = jnp.zeros_like(entries[0][0])
    upper_r = []
    for row_idx in range(order_n):
        upper_r.append([zero_entry] * order_n)
    for row_idx in range(order_n):
        running = entries[row_idx][row_idx]
        for earlier in range(row_idx):
            running = running - upper_r[earlier][row_idx] * upper_r[earlier][row_idx]
        pivot_val = jnp.sqrt(running)
        upper_r[row_idx][row_idx] = pivot_val
        for col_idx in range(row_idx + 1, order_n):
            entry_val = entries[row_idx][col_idx]
            for earlier in range(row_idx):
                entry_val = entry_val - upper_r[earlier][row_idx] * upper_r[earlier][col_idx]
            upper_r[row_idx][col_idx] = entry_val / pivot_val
    return upper_r


def small_update(gram_sum, scale_factor, depth_n):
    order_n = depth_n + 1
    entries = gram_sum
    upper_r = cholesky_upper(entries, order_n)
    shifted = [
        [
            SHIFT * upper_r[row_idx][col_idx] + upper_r[row_idx][col_idx + 1]
            for col_idx in range(depth_n)
        ]
        for row_idx in range(order_n)
    ]
    hessen = []
    for row_idx in range(order_n):
        row_vals = []
        for col_idx in range(depth_n):
            entry_val = shifted[row_idx][col_idx]
            for earlier in range(col_idx):
                entry_val = entry_val - row_vals[earlier] * upper_r[earlier][col_idx]
            row_vals.append(entry_val / upper_r[col_idx][col_idx])
        hessen.append(row_vals)
    normal = []
    for row_idx in range(depth_n):
        row_vals = []
        for col_idx in range(depth_n):
            entry_val = hessen[0][row_idx] * hessen[0][col_idx]
            for inner in range(1, order_n):
                entry_val = entry_val + hessen[inner][row_idx] * hessen[inner][col_idx]
            row_vals.append(entry_val)
        normal.append(row_vals)
    target = [scale_factor * upper_r[0][0] * hessen[0][col_idx] for col_idx in range(depth_n)]
    factor = cholesky_upper(normal, depth_n)
    forward = []
    for row_idx in range(depth_n):
        entry_val = target[row_idx]
        for earlier in range(row_idx):
            entry_val = entry_val - factor[earlier][row_idx] * forward[earlier]
        forward.append(entry_val / factor[row_idx][row_idx])
    solved = [None] * depth_n
    for row_idx in range(depth_n - 1, -1, -1):
        entry_val = forward[row_idx]
        for later in range(row_idx + 1, depth_n):
            entry_val = entry_val - factor[row_idx][later] * solved[later]
        solved[row_idx] = entry_val / factor[row_idx][row_idx]
    weights = [None] * depth_n
    for row_idx in range(depth_n - 1, -1, -1):
        entry_val = solved[row_idx]
        for later in range(row_idx + 1, depth_n):
            entry_val = entry_val - upper_r[row_idx][later] * weights[later]
        weights[row_idx] = entry_val / upper_r[row_idx][row_idx]
    return (hessen, weights)


def dot(left, right):
    return jnp.dot(left, right, precision=HIGH, preferred_element_type=jnp.float32)


def lane_group(shape):
    return lax.broadcasted_iota(jnp.int32, shape, 1) // WIDTH


def pack(pieces):
    group = lane_group(pieces[0].shape)
    out = pieces[0]
    for q in range(1, len(pieces)):
        out = jnp.where(group == q, pltpu.roll(pieces[q], q * WIDTH, 1), out)
    return out


def lanes_to_front(value, q):
    return value if q == 0 else pltpu.roll(value, LANES - q * WIDTH, 1)


def kernel(
    lists, res, sol, near, coup, cb, rbt, out, hout,
    W, T, U, HP, HB, H, F, NB, CP, GR, GZ, GY, GC, WF, XH, IV, IX,
    z_send, z_recv, y_send, y_recv, c_send, c_recv, h_send, h_recv,
    n_send, n_recv, p_send, p_recv, o_send, o_recv, q_send, q_recv,
    i_send, i_recv, i_copy,
):
    row = lax.axis_index("row")
    col = lax.axis_index("col")
    core = row % NC
    zz = (row // NC) % NZ
    yy = row // (NC * NZ)
    z_dev = [(yy * NZ + (zz + d) % NZ) * NC + core for d in range(NZ)]
    y_dev = [(((yy + d) % NY) * NZ + zz) * NC + core for d in range(NY)]
    mate = row + 1 - 2 * core
    above = (row + 1) % NROW
    below = (row + NROW - 1) % NROW
    x_dev = [(col + d) % NX for d in range(NX)]

    barrier = pltpu.get_barrier_semaphore()
    for dev in z_dev[1:] + y_dev[1:] + [mate, above, below]:
        pl.semaphore_signal(barrier, inc=1, device_id={"row": dev}, device_id_type=MESH)
    for dev in x_dev[1:]:
        pl.semaphore_signal(barrier, inc=1, device_id={"col": dev}, device_id_type=MESH)

    def to_row(src, dst, send, recv, dev):
        return pltpu.make_async_remote_copy(
            src_ref=src, dst_ref=dst, send_sem=send, recv_sem=recv,
            device_id={"row": dev}, device_id_type=MESH,
        )

    def to_col(src, dst, send, recv, dev):
        return pltpu.make_async_remote_copy(
            src_ref=src, dst_ref=dst, send_sem=send, recv_sem=recv,
            device_id={"col": dev}, device_id_type=MESH,
        )

    W[0] = pltpu.roll(res[...], (LANES - col * WIDTH) % LANES, 1)

    def stage_table(k):
        pieces = []
        for c in range(CL_DEV):
            value = dot(cb[c], W[k, pl.ds(c * LEAF_UNKNOWNS, LEAF_UNKNOWNS), :])
            pieces += [value[0:8], value[8:16]]
        T[k, 0, 0, 0] = pack(pieces)

    def stage_halo(k):
        HP[k, 0] = pack([W[k, pl.ds(q * LANES, LANES), :] for q in range(4)])

    stage_table(0)
    stage_halo(0)
    W[1] = jnp.zeros((ROWS, LANES), jnp.float32)
    pl.semaphore_wait(barrier, (NZ - 1) + (NY - 1) + 3 + (NX - 1))

    right, left = x_dev[1], x_dev[NX - 1]

    def near_copy(n, src, dst, dev):
        return to_col(src, dst, n_send.at[n], n_recv.at[n], dev)

    near_first = [
        near_copy(0, near.at[0], NB.at[0, 0], right),
        near_copy(1, near.at[1], NB.at[2, 1], left),
    ]
    near_second = [
        near_copy(2, near.at[1], NB.at[0, 1], right),
        near_copy(3, near.at[0], NB.at[2, 0], left),
    ]
    near_relay = [
        near_copy(4, NB.at[0, 0], NB.at[1, 0], right),
        near_copy(5, NB.at[2, 1], NB.at[1, 1], left),
    ]
    list_out = [
        to_col(lists, IV.at[d - 1], i_send.at[d - 1], i_recv.at[d - 1], x_dev[d])
        for d in range(1, NX)
    ]
    list_in = [
        pltpu.make_async_copy(lists if d == 0 else IV.at[d - 1], IX.at[d], i_copy.at[d])
        for d in range(NX)
    ]
    coup_out = [
        to_col(coup, CP.at[d - 1], p_send.at[d - 1], p_recv.at[d - 1], x_dev[d])
        for d in range(1, NX)
    ]

    def unpack_table(k, side, run):
        def one(n, carry):
            for y in range(NY):
                value = T[k, side, y, n]
                for q in range(4):
                    where = ((side * NY + y) * NZ + n) * CL_DEV + q // 2
                    U[where, pl.ds((q % 2) * 8, 8), :] = lanes_to_front(value, q)
            return carry

        lax.fori_loop(run[0], run[1], one, 0)

    def panel_copies(k):
        return [
            to_col(
                HP.at[k, 0], HP.at[k, d], o_send.at[k - 1, d - 1], o_recv.at[k - 1, d - 1], x_dev[d]
            )
            for d in range(1, NX)
        ]

    def near_product(k, more):
        for q in range(4):
            rows = pl.ds((q % 2) * LANES, LANES)
            H[q // 2, rows, :] = lanes_to_front(HB[k, 0], q)
            H[4 + q // 2, rows, :] = lanes_to_front(HB[k, 1], q)
        for c in range(CL_DEV):
            H[2 + c] = W[k, pl.ds(c * LEAF_UNKNOWNS, LEAF_UNKNOWNS), :]
        for c in range(CL_DEV):
            total = dot(near[c], H[IX[0, c, SLOTS]])
            for s in range(1, NX):
                total = total + dot(NB[s - 1, c], H[IX[s, c, SLOTS]])
            rows = pl.ds(c * LEAF_UNKNOWNS, LEAF_UNKNOWNS)
            W[k + 1, rows, :] = W[k + 1, rows, :] + total if more else total

    def step(k, carry):
        z_out = [
            to_row(
                T.at[k, 0, 0, 0], T.at[k, 0, 0, d], z_send.at[k],
                z_recv.at[k, [d >= lo and d < hi for lo, hi in RUNS].index(True)], z_dev[d],
            )
            for d in sorted(range(1, NZ), key=lambda d: -min(d, NZ - d))
        ]
        z_all = to_row(
            T.at[k, 0, 0, pl.ds(1, NZ - 1)], T.at[k, 0, 0, pl.ds(1, NZ - 1)],
            z_send.at[k], z_recv.at[k, 0], z_dev[1],
        )
        z_in, y_out, c_out = [], [], []
        for n, (lo, hi) in enumerate(RUNS):
            got = pl.ds(max(lo, 1), hi - max(lo, 1))
            z_in.append(
                to_row(T.at[k, 0, 0, got], T.at[k, 0, 0, got], z_send.at[k], z_recv.at[k, n], z_dev[1])
                if hi > 1 else None
            )
            run = pl.ds(lo, hi - lo)
            y_out.append([
                to_row(
                    T.at[k, 0, 0, run], T.at[k, 0, d, run],
                    y_send.at[k, n, d - 1], y_recv.at[k, n, d - 1], y_dev[d],
                )
                for d in range(1, NY)
            ])
            c_out.append(
                to_row(
                    T.at[k, 0, :, run], T.at[k, 1, :, run], c_send.at[k, n], c_recv.at[k, n], mate
                )
            )
        halo_out = [
            to_row(HP.at[k, 0], HB.at[k, 0], h_send.at[k, 0], h_recv.at[k, 0], above),
            to_row(HP.at[k, 0], HB.at[k, 1], h_send.at[k, 1], h_recv.at[k, 1], below),
        ]
        for copy in z_out:
            copy.start()
        for copy in halo_out:
            copy.start()

        @pl.when(k == 0)
        def _():
            for copy in near_first + list_out + coup_out + near_second:
                copy.start()

        for copy in halo_out:
            copy.wait()

        @pl.when(k > 0)
        def _():
            for copy in panel_copies(k):
                copy.start()

        for n in range(len(RUNS)):
            if n == len(RUNS) - 1:

                @pl.when(k > 0)
                def _():
                    near_product(k, False)

            if z_in[n] is not None:
                z_in[n].wait_recv()
            for copy in y_out[n]:
                copy.start()

        @pl.when(k == 0)
        def _():
            for copy, relay in zip(near_first, near_relay):
                copy.wait_recv()
                relay.start()
            for copy in list_out:
                copy.wait()
            for copy in list_in:
                copy.start()

        for n, run in enumerate(RUNS):
            for copy in y_out[n]:
                copy.wait_recv()
            c_out[n].start()
            unpack_table(k, 0, run)

        @pl.when(k == 0)
        def _():
            for copy in list_in:
                copy.wait()
            for copy in coup_out:
                copy.wait()

        for n, run in enumerate(RUNS):
            c_out[n].wait_recv()
            unpack_table(k, 1, run)
        z_all.wait_send()
        for n in range(len(RUNS)):
            for copy in y_out[n]:
                copy.wait_send()
            c_out[n].wait_send()

        for c in range(CL_DEV):
            for s in range(NX):

                def fetch(p, carry, c=c, s=s):
                    F[c, pl.ds((s * SLOTS + p) * RANK, RANK), :] = U[IX[s, c, p]]
                    return carry

                lax.fori_loop(0, SLOTS, fetch, 0, unroll=8)
        span = SLOTS * RANK
        for c in range(CL_DEV):
            rows = pl.ds(c * RANK, RANK)
            total = dot(coup[rows, :], F[c, pl.ds(0, span), :])
            for s in range(1, NX):
                total = total + dot(CP[s - 1, rows, :], F[c, pl.ds(s * span, span), :])
            W[k + 1, pl.ds(c * LEAF_UNKNOWNS, LEAF_UNKNOWNS), :] += dot(rbt[c], total)

        @pl.when(k == 0)
        def _():
            for copy in near_first:
                copy.wait_send()
            for copy in near_second + near_relay:
                copy.wait()
            near_product(k, True)

        @pl.when(k < SB - 1)
        def _():
            stage_table(k + 1)
            stage_halo(k + 1)

        return carry

    lax.fori_loop(0, SB, step, 0)

    chunk = 32

    def gather_gram(n, sums):
        vals = [W[a, pl.ds(n * chunk, chunk), :] for a in range(SB + 1)]
        new = []
        for (a, b), old in zip(PAIRS, sums):
            prod = vals[a] * vals[b]
            new.append(old + ((prod[0:8] + prod[8:16]) + (prod[16:24] + prod[24:32])))
        return tuple(new)

    sums = lax.fori_loop(
        0, ROWS // chunk, gather_gram, tuple(jnp.zeros((8, LANES), jnp.float32) for _ in PAIRS)
    )
    GR[...] = jnp.zeros_like(GR)
    for n, value in enumerate(sums):
        GR[pl.ds(n, 1), :] = jnp.sum(value, axis=0, keepdims=True)
    grams = GR[...]
    GZ[0] = pack([grams[0:8], grams[8:16]])
    z_out = [
        to_row(GZ.at[0], GZ.at[d], z_send.at[SB], z_recv.at[SB, 0], z_dev[d]) for d in range(1, NZ)
    ]
    z_all = to_row(
        GZ.at[pl.ds(1, NZ - 1)], GZ.at[pl.ds(1, NZ - 1)], z_send.at[SB], z_recv.at[SB, 0], z_dev[1]
    )
    for copy in z_out:
        copy.start()
    group = lane_group((LANES, LANES))
    for k in range(1, SB):
        for copy in panel_copies(k):
            copy.wait()
        for q in range(4):
            full = lanes_to_front(HP[k, col % NX], q)
            for src in range(1, NX):
                moved = HP[k, (col + NX - src) % NX]
                if src != q:
                    moved = pltpu.roll(moved, ((src - q) * WIDTH) % LANES, 1)
                full = jnp.where(group == src, moved, full)
            WF[k - 1, pl.ds(q * LANES, LANES), :] = full
    z_all.wait()
    total = GZ[zz % NZ]
    for src in range(1, NZ):
        total = total + GZ[(zz + NZ - src) % NZ]
    GY[0] = total
    y_out = [
        to_row(GY.at[0], GY.at[d], y_send.at[SB, 0, d - 1], y_recv.at[SB, 0, d - 1], y_dev[d])
        for d in range(1, NY)
    ]
    for copy in y_out:
        copy.start()
    for copy in y_out:
        copy.wait()
    total = GY[yy % NY]
    for src in range(1, NY):
        total = total + GY[(yy + NY - src) % NY]
    GC[0] = total
    c_out = to_row(GC.at[0], GC.at[1], c_send.at[SB, 0], c_recv.at[SB, 0], mate)
    c_out.start()
    c_out.wait()
    total = GC[0] + GC[1]
    second = lanes_to_front(total, 1)
    gram = [[None] * (SB + 1) for _ in range(SB + 1)]
    for n, (a, b) in enumerate(PAIRS):
        gram[a][b] = gram[b][a] = total[n : n + 1] if n < 8 else second[n - 8 : n - 7]
    hessen, weights = small_update(gram, 1.0, SB)
    for a in range(SB + 1):
        for b in range(SB):
            XH[0, pl.ds(a * SB + b, 1), :] = hessen[a][b]
    for k in range(SB):
        XH[0, pl.ds((SB + 1) * SB + k, 1), :] = weights[k]
    last = [
        to_col(XH.at[0], XH.at[d], q_send.at[d - 1], q_recv.at[d - 1], x_dev[d])
        for d in range(1, NX)
    ]
    for copy in last:
        copy.start()
    for copy in last:
        copy.wait()
    both = pack([XH[(col + NX - src) % NX] for src in range(NX)])
    hout[...] = both
    full = [both[(SB + 1) * SB + k : (SB + 1) * SB + k + 1] for k in range(SB)]
    for q in range(4):
        rows = pl.ds(q * LANES, LANES)
        value = sol[rows, :] + full[0] * res[rows, :]
        for k in range(1, SB):
            value = value + full[k] * WF[k - 1, rows, :]
        out[rows, :] = value


def local(
    residual,
    solution,
    near_field_blocks,
    near_cols,
    couplings,
    far_cols,
    far_count,
    col_basis,
    row_basis,
):
    row = lax.axis_index("row")
    col = lax.axis_index("col")
    positions = col * SLOTS + jnp.arange(SLOTS, dtype=jnp.int32)
    live = positions[None, :] < far_count[:, None]
    weighted = jnp.where(live[:, :, None, None], couplings, 0.0)
    weighted = weighted.transpose(0, 2, 1, 3).reshape(CL_DEV * RANK, SLOTS * RANK)
    owner = far_cols // CL_DEV
    core, rest = owner % NC, owner // NC
    tile = (
        ((row + NC - core) % NC) * (NY * NZ)
        + ((row // (NC * NZ) + NY - rest // NZ) % NY) * NZ
        + (row // NC + NZ - rest % NZ) % NZ
    )
    lists = jnp.concatenate(
        [tile * CL_DEV + far_cols % CL_DEV, near_cols - (row * CL_DEV - REACH)], axis=1
    ).astype(jnp.int32)
    lists = jnp.pad(lists, ((0, 8 - CL_DEV), (0, LANES - SLOTS - 1)))
    f32 = jnp.float32
    vmem = pl.BlockSpec(memory_space=pltpu.VMEM)
    dma = pltpu.SemaphoreType.DMA
    new_sol, hess = pl.pallas_call(
        kernel,
        out_shape=(
            jax.ShapeDtypeStruct((ROWS, LANES), f32),
            jax.ShapeDtypeStruct((24, LANES), f32),
        ),
        in_specs=[vmem] * 7,
        out_specs=(vmem, vmem),
        scratch_shapes=[
            pltpu.VMEM((SB + 1, ROWS, LANES), f32),
            pltpu.VMEM((SB, NC, NY, NZ, 8, LANES), f32),
            pltpu.VMEM((NROW * CL_DEV, RANK, LANES), f32),
            pltpu.VMEM((SB, NX, LANES, LANES), f32),
            pltpu.VMEM((SB, 2, LANES, LANES), f32),
            pltpu.VMEM((CL_DEV + 2 * REACH, LEAF_UNKNOWNS, LANES), f32),
            pltpu.VMEM((CL_DEV, FAR * RANK, LANES), f32),
            pltpu.VMEM((NX - 1, CL_DEV, LEAF_UNKNOWNS, LEAF_UNKNOWNS), f32),
            pltpu.VMEM((NX - 1, CL_DEV * RANK, SLOTS * RANK), f32),
            pltpu.VMEM((16, LANES), f32),
            pltpu.VMEM((NZ, 8, LANES), f32),
            pltpu.VMEM((NY, 8, LANES), f32),
            pltpu.VMEM((NC, 8, LANES), f32),
            pltpu.VMEM((SB - 1, ROWS, LANES), f32),
            pltpu.VMEM((NX, 24, LANES), f32),
            pltpu.VMEM((NX - 1, 8, LANES), jnp.int32),
            pltpu.SMEM((NX, 8, LANES), jnp.int32),
            dma((SB + 1,)), dma((SB + 1, len(RUNS))),
            dma((SB + 1, len(RUNS), NY - 1)), dma((SB + 1, len(RUNS), NY - 1)),
            dma((SB + 1, len(RUNS))), dma((SB + 1, len(RUNS))),
            dma((SB, 2)), dma((SB, 2)),
            dma((6,)), dma((6,)),
            dma((NX - 1,)), dma((NX - 1,)),
            dma((SB - 1, NX - 1)), dma((SB - 1, NX - 1)),
            dma((NX - 1,)), dma((NX - 1,)),
            dma((NX - 1,)), dma((NX - 1,)), dma((NX,)),
        ],
        compiler_params=pltpu.CompilerParams(
            collective_id=0, has_side_effects=True, vmem_limit_bytes=48 * 1024 * 1024
        ),
    )(
        lists,
        residual,
        solution,
        near_field_blocks.reshape(CL_DEV, LEAF_UNKNOWNS, LEAF_UNKNOWNS),
        weighted,
        col_basis,
        row_basis.transpose(0, 2, 1),
    )
    return (new_sol, hess[: (SB + 1) * SB].reshape(SB + 1, SB, LANES))


def solution(mesh):
    placed = (
        P("row", None),
        P("row", None),
        P("row", "col", None, None),
        P("row", "col"),
        P("row", "col", None, None),
        P("row", "col"),
        P("row"),
        P("row", None, None),
        P("row", None, None),
    )
    return jax.shard_map(
        local, mesh=mesh, in_specs=placed, out_specs=(P("row", None), P()), check_vma=False
    )
```

```python
import functools

import jax
import jax.numpy as jnp
from jax import lax
from jax.experimental import pallas as pl
from jax.experimental.pallas import tpu as pltpu
from jax.sharding import PartitionSpec as P

LEAF_UNKNOWNS = 256
CL_DEV = 2
REACH = 2
SB = 4
RANK = 16
LANES = 128
NY, NZ, NC = 4, 16, 2
NX = 4
NROW = NY * NZ * NC
WIDTH = LANES // NX
ROWS = CL_DEV * LEAF_UNKNOWNS
SLOTS = 16
FAR = SLOTS * NX
REACH_Z = NZ // 4
RUNS = [
    run
    for run in ((0, REACH_Z + 1), (NZ - REACH_Z, NZ), (REACH_Z + 1, NZ - REACH_Z))
    if run[1] > run[0]
]
PAIRS = [(a, b) for a in range(SB + 1) for b in range(a, SB + 1)]


HIGH = lax.Precision.HIGH
SHIFT = 1.0
MESH = pl.DeviceIdType.MESH


def cholesky_upper(entries, order_n):
    zero_entry = jnp.zeros_like(entries[0][0])
    upper_r = []
    for row_idx in range(order_n):
        upper_r.append([zero_entry] * order_n)
    for row_idx in range(order_n):
        running = entries[row_idx][row_idx]
        for earlier in range(row_idx):
            running = running - upper_r[earlier][row_idx] * upper_r[earlier][row_idx]
        pivot_val = jnp.sqrt(running)
        upper_r[row_idx][row_idx] = pivot_val
        for col_idx in range(row_idx + 1, order_n):
            entry_val = entries[row_idx][col_idx]
            for earlier in range(row_idx):
                entry_val = entry_val - upper_r[earlier][row_idx] * upper_r[earlier][col_idx]
            upper_r[row_idx][col_idx] = entry_val / pivot_val
    return upper_r


def small_update(gram_sum, scale_factor, depth_n):
    order_n = depth_n + 1
    entries = gram_sum
    upper_r = cholesky_upper(entries, order_n)
    shifted = [
        [
            SHIFT * upper_r[row_idx][col_idx] + upper_r[row_idx][col_idx + 1]
            for col_idx in range(depth_n)
        ]
        for row_idx in range(order_n)
    ]
    hessen = []
    for row_idx in range(order_n):
        row_vals = []
        for col_idx in range(depth_n):
            entry_val = shifted[row_idx][col_idx]
            for earlier in range(col_idx):
                entry_val = entry_val - row_vals[earlier] * upper_r[earlier][col_idx]
            row_vals.append(entry_val / upper_r[col_idx][col_idx])
        hessen.append(row_vals)
    normal = []
    for row_idx in range(depth_n):
        row_vals = []
        for col_idx in range(depth_n):
            entry_val = hessen[0][row_idx] * hessen[0][col_idx]
            for inner in range(1, order_n):
                entry_val = entry_val + hessen[inner][row_idx] * hessen[inner][col_idx]
            row_vals.append(entry_val)
        normal.append(row_vals)
    target = [scale_factor * upper_r[0][0] * hessen[0][col_idx] for col_idx in range(depth_n)]
    factor = cholesky_upper(normal, depth_n)
    forward = []
    for row_idx in range(depth_n):
        entry_val = target[row_idx]
        for earlier in range(row_idx):
            entry_val = entry_val - factor[earlier][row_idx] * forward[earlier]
        forward.append(entry_val / factor[row_idx][row_idx])
    solved = [None] * depth_n
    for row_idx in range(depth_n - 1, -1, -1):
        entry_val = forward[row_idx]
        for later in range(row_idx + 1, depth_n):
            entry_val = entry_val - factor[row_idx][later] * solved[later]
        solved[row_idx] = entry_val / factor[row_idx][row_idx]
    weights = [None] * depth_n
    for row_idx in range(depth_n - 1, -1, -1):
        entry_val = solved[row_idx]
        for later in range(row_idx + 1, depth_n):
            entry_val = entry_val - upper_r[row_idx][later] * weights[later]
        weights[row_idx] = entry_val / upper_r[row_idx][row_idx]
    return (hessen, weights)


def dot(left, right):
    return jnp.dot(left, right, precision=HIGH, preferred_element_type=jnp.float32)


def lane_group(shape):
    return lax.broadcasted_iota(jnp.int32, shape, 1) // WIDTH


def pack(pieces):
    group = lane_group(pieces[0].shape)
    out = pieces[0]
    for q in range(1, len(pieces)):
        out = jnp.where(group == q, pltpu.roll(pieces[q], q * WIDTH, 1), out)
    return out


def lanes_to_front(value, q):
    return value if q == 0 else pltpu.roll(value, LANES - q * WIDTH, 1)


def kernel(
    lists, res, sol, near, coup, cb, rbt, out, hout,
    W, T, U, HP, HB, H, F, NB, CP, GR, GZ, GY, GC, WF, XH, IV, IX,
    z_send, z_recv, y_send, y_recv, c_send, c_recv, h_send, h_recv,
    n_send, n_recv, p_send, p_recv, o_send, o_recv, q_send, q_recv,
    i_send, i_recv, i_copy,
):
    row = lax.axis_index("row")
    col = lax.axis_index("col")
    core = row % NC
    zz = (row // NC) % NZ
    yy = row // (NC * NZ)
    z_dev = [(yy * NZ + (zz + d) % NZ) * NC + core for d in range(NZ)]
    y_dev = [(((yy + d) % NY) * NZ + zz) * NC + core for d in range(NY)]
    mate = row + 1 - 2 * core
    above = (row + 1) % NROW
    below = (row + NROW - 1) % NROW
    x_dev = [(col + d) % NX for d in range(NX)]

    barrier = pltpu.get_barrier_semaphore()
    for dev in z_dev[1:] + y_dev[1:] + [mate, above, below]:
        pl.semaphore_signal(barrier, inc=1, device_id={"row": dev}, device_id_type=MESH)
    for dev in x_dev[1:]:
        pl.semaphore_signal(barrier, inc=1, device_id={"col": dev}, device_id_type=MESH)

    def to_row(src, dst, send, recv, dev):
        return pltpu.make_async_remote_copy(
            src_ref=src, dst_ref=dst, send_sem=send, recv_sem=recv,
            device_id={"row": dev}, device_id_type=MESH,
        )

    def to_col(src, dst, send, recv, dev):
        return pltpu.make_async_remote_copy(
            src_ref=src, dst_ref=dst, send_sem=send, recv_sem=recv,
            device_id={"col": dev}, device_id_type=MESH,
        )

    W[0] = pltpu.roll(res[...], (LANES - col * WIDTH) % LANES, 1)

    def stage_table(k):
        pieces = []
        for c in range(CL_DEV):
            value = dot(cb[c], W[k, pl.ds(c * LEAF_UNKNOWNS, LEAF_UNKNOWNS), :])
            pieces += [value[0:8], value[8:16]]
        T[k, 0, 0, 0] = pack(pieces)

    def stage_halo(k):
        HP[k, 0] = pack([W[k, pl.ds(q * LANES, LANES), :] for q in range(4)])

    stage_table(0)
    stage_halo(0)
    W[1] = jnp.zeros((ROWS, LANES), jnp.float32)
    pl.semaphore_wait(barrier, (NZ - 1) + (NY - 1) + 3 + (NX - 1))

    right, left = x_dev[1], x_dev[NX - 1]

    def near_copy(n, src, dst, dev):
        return to_col(src, dst, n_send.at[n], n_recv.at[n], dev)

    near_first = [
        near_copy(0, near.at[0], NB.at[0, 0], right),
        near_copy(1, near.at[1], NB.at[2, 1], left),
    ]
    near_second = [
        near_copy(2, near.at[1], NB.at[0, 1], right),
        near_copy(3, near.at[0], NB.at[2, 0], left),
    ]
    near_relay = [
        near_copy(4, NB.at[0, 0], NB.at[1, 0], right),
        near_copy(5, NB.at[2, 1], NB.at[1, 1], left),
    ]
    list_out = [
        to_col(lists, IV.at[d - 1], i_send.at[d - 1], i_recv.at[d - 1], x_dev[d])
        for d in range(1, NX)
    ]
    list_in = [
        pltpu.make_async_copy(lists if d == 0 else IV.at[d - 1], IX.at[d], i_copy.at[d])
        for d in range(NX)
    ]
    coup_out = [
        to_col(coup, CP.at[d - 1], p_send.at[d - 1], p_recv.at[d - 1], x_dev[d])
        for d in range(1, NX)
    ]

    def unpack_table(k, side, run):
        def one(n, carry):
            for y in range(NY):
                value = T[k, side, y, n]
                for q in range(4):
                    where = ((side * NY + y) * NZ + n) * CL_DEV + q // 2
                    U[where, pl.ds((q % 2) * 8, 8), :] = lanes_to_front(value, q)
            return carry

        lax.fori_loop(run[0], run[1], one, 0)

    def panel_copies(k):
        return [
            to_col(
                HP.at[k, 0], HP.at[k, d], o_send.at[k - 1, d - 1], o_recv.at[k - 1, d - 1], x_dev[d]
            )
            for d in range(1, NX)
        ]

    def near_panels(k):
        for q in range(4):
            rows = pl.ds((q % 2) * LANES, LANES)
            H[q // 2, rows, :] = lanes_to_front(HB[k, 0], q)
            H[4 + q // 2, rows, :] = lanes_to_front(HB[k, 1], q)
        for c in range(CL_DEV):
            H[2 + c] = W[k, pl.ds(c * LEAF_UNKNOWNS, LEAF_UNKNOWNS), :]

    def near_product(k, more, slots):
        for c in range(CL_DEV):
            total = None
            for s in slots:
                term = dot(near[c] if s == 0 else NB[s - 1, c], H[IX[s, c, SLOTS]])
                total = term if total is None else total + term
            rows = pl.ds(c * LEAF_UNKNOWNS, LEAF_UNKNOWNS)
            W[k + 1, rows, :] = W[k + 1, rows, :] + total if more else total

    def step(k, carry):
        z_out = [
            to_row(
                T.at[k, 0, 0, 0], T.at[k, 0, 0, d], z_send.at[k],
                z_recv.at[k, [d >= lo and d < hi for lo, hi in RUNS].index(True)], z_dev[d],
            )
            for d in sorted(range(1, NZ), key=lambda d: -min(d, NZ - d))
        ]
        z_all = to_row(
            T.at[k, 0, 0, pl.ds(1, NZ - 1)], T.at[k, 0, 0, pl.ds(1, NZ - 1)],
            z_send.at[k], z_recv.at[k, 0], z_dev[1],
        )
        z_in, y_out, c_out = [], [], []
        for n, (lo, hi) in enumerate(RUNS):
            got = pl.ds(max(lo, 1), hi - max(lo, 1))
            z_in.append(
                to_row(T.at[k, 0, 0, got], T.at[k, 0, 0, got], z_send.at[k], z_recv.at[k, n], z_dev[1])
                if hi > 1 else None
            )
            run = pl.ds(lo, hi - lo)
            y_out.append([
                to_row(
                    T.at[k, 0, 0, run], T.at[k, 0, d, run],
                    y_send.at[k, n, d - 1], y_recv.at[k, n, d - 1], y_dev[d],
                )
                for d in range(1, NY)
            ])
            c_out.append(
                to_row(
                    T.at[k, 0, :, run], T.at[k, 1, :, run], c_send.at[k, n], c_recv.at[k, n], mate
                )
            )
        halo_out = [
            to_row(HP.at[k, 0], HB.at[k, 0], h_send.at[k, 0], h_recv.at[k, 0], above),
            to_row(HP.at[k, 0], HB.at[k, 1], h_send.at[k, 1], h_recv.at[k, 1], below),
        ]
        for copy in z_out:
            copy.start()
        for copy in halo_out:
            copy.start()

        @pl.when(k == 0)
        def _():
            for copy in near_first + list_out + coup_out + near_second:
                copy.start()

        for copy in halo_out:
            copy.wait()

        @pl.when(k > 0)
        def _():
            for copy in panel_copies(k):
                copy.start()

        for n in range(len(RUNS)):
            if n == len(RUNS) - 1:

                @pl.when(k > 0)
                def _():
                    near_panels(k)
                    near_product(k, False, range(NX))

            if z_in[n] is not None:
                z_in[n].wait_recv()
            for copy in y_out[n]:
                copy.start()

        @pl.when(k == 0)
        def _():
            for copy, relay in zip(near_first, near_relay):
                copy.wait_recv()
                relay.start()
            for copy in list_out:
                copy.wait()
            for copy in list_in:
                copy.start()

        for n, run in enumerate(RUNS):
            for copy in y_out[n]:
                copy.wait_recv()
            c_out[n].start()
            unpack_table(k, 0, run)

        @pl.when(k == 0)
        def _():
            for copy in list_in:
                copy.wait()
            for copy in coup_out:
                copy.wait()

        for n, run in enumerate(RUNS):
            c_out[n].wait_recv()
            unpack_table(k, 1, run)
        z_all.wait_send()
        for n in range(len(RUNS)):
            for copy in y_out[n]:
                copy.wait_send()
            c_out[n].wait_send()

        for c in range(CL_DEV):
            for s in range(NX):

                def fetch(p, carry, c=c, s=s):
                    F[c, pl.ds((s * SLOTS + p) * RANK, RANK), :] = U[IX[s, c, p]]
                    return carry

                lax.fori_loop(0, SLOTS, fetch, 0, unroll=8)
        span = SLOTS * RANK
        for c in range(CL_DEV):
            rows = pl.ds(c * RANK, RANK)
            total = dot(coup[rows, :], F[c, pl.ds(0, span), :])
            for s in range(1, NX):
                total = total + dot(CP[s - 1, rows, :], F[c, pl.ds(s * span, span), :])
            W[k + 1, pl.ds(c * LEAF_UNKNOWNS, LEAF_UNKNOWNS), :] += dot(rbt[c], total)

        @pl.when(k == 0)
        def _():
            near_panels(k)
            for copy in near_first:
                copy.wait_send()
            for copy in near_second:
                copy.wait()
            near_product(k, True, (0, 1, 3))
            for copy in near_relay:
                copy.wait()
            near_product(k, True, (2,))

        @pl.when(k < SB - 1)
        def _():
            stage_table(k + 1)
            stage_halo(k + 1)

        return carry

    lax.fori_loop(0, SB, step, 0)

    chunk = 32

    def gather_gram(n, sums):
        vals = [W[a, pl.ds(n * chunk, chunk), :] for a in range(SB + 1)]
        new = []
        for (a, b), old in zip(PAIRS, sums):
            prod = vals[a] * vals[b]
            new.append(old + ((prod[0:8] + prod[8:16]) + (prod[16:24] + prod[24:32])))
        return tuple(new)

    sums = lax.fori_loop(
        0, ROWS // chunk, gather_gram, tuple(jnp.zeros((8, LANES), jnp.float32) for _ in PAIRS)
    )
    GR[...] = jnp.zeros_like(GR)
    for n, value in enumerate(sums):
        GR[pl.ds(n, 1), :] = jnp.sum(value, axis=0, keepdims=True)
    grams = GR[...]
    GZ[0] = pack([grams[0:8], grams[8:16]])
    z_out = [
        to_row(GZ.at[0], GZ.at[d], z_send.at[SB], z_recv.at[SB, 0], z_dev[d]) for d in range(1, NZ)
    ]
    z_all = to_row(
        GZ.at[pl.ds(1, NZ - 1)], GZ.at[pl.ds(1, NZ - 1)], z_send.at[SB], z_recv.at[SB, 0], z_dev[1]
    )
    for copy in z_out:
        copy.start()
    group = lane_group((LANES, LANES))
    for k in range(1, SB):
        for copy in panel_copies(k):
            copy.wait()
        for q in range(4):
            full = lanes_to_front(HP[k, col % NX], q)
            for src in range(1, NX):
                moved = HP[k, (col + NX - src) % NX]
                if src != q:
                    moved = pltpu.roll(moved, ((src - q) * WIDTH) % LANES, 1)
                full = jnp.where(group == src, moved, full)
            WF[k - 1, pl.ds(q * LANES, LANES), :] = full
    z_all.wait()
    total = GZ[zz % NZ]
    for src in range(1, NZ):
        total = total + GZ[(zz + NZ - src) % NZ]
    GY[0] = total
    y_out = [
        to_row(GY.at[0], GY.at[d], y_send.at[SB, 0, d - 1], y_recv.at[SB, 0, d - 1], y_dev[d])
        for d in range(1, NY)
    ]
    for copy in y_out:
        copy.start()
    for copy in y_out:
        copy.wait()
    total = GY[yy % NY]
    for src in range(1, NY):
        total = total + GY[(yy + NY - src) % NY]
    GC[0] = total
    c_out = to_row(GC.at[0], GC.at[1], c_send.at[SB, 0], c_recv.at[SB, 0], mate)
    c_out.start()
    c_out.wait()
    total = GC[0] + GC[1]
    second = lanes_to_front(total, 1)
    gram = [[None] * (SB + 1) for _ in range(SB + 1)]
    for n, (a, b) in enumerate(PAIRS):
        gram[a][b] = gram[b][a] = total[n : n + 1] if n < 8 else second[n - 8 : n - 7]
    hessen, weights = small_update(gram, 1.0, SB)
    for a in range(SB + 1):
        for b in range(SB):
            XH[0, pl.ds(a * SB + b, 1), :] = hessen[a][b]
    for k in range(SB):
        XH[0, pl.ds((SB + 1) * SB + k, 1), :] = weights[k]
    last = [
        to_col(XH.at[0], XH.at[d], q_send.at[d - 1], q_recv.at[d - 1], x_dev[d])
        for d in range(1, NX)
    ]
    for copy in last:
        copy.start()
    for copy in last:
        copy.wait()
    both = pack([XH[(col + NX - src) % NX] for src in range(NX)])
    hout[...] = both
    full = [both[(SB + 1) * SB + k : (SB + 1) * SB + k + 1] for k in range(SB)]
    for q in range(4):
        rows = pl.ds(q * LANES, LANES)
        value = sol[rows, :] + full[0] * res[rows, :]
        for k in range(1, SB):
            value = value + full[k] * WF[k - 1, rows, :]
        out[rows, :] = value


def local(
    residual,
    solution,
    near_field_blocks,
    near_cols,
    couplings,
    far_cols,
    far_count,
    col_basis,
    row_basis,
):
    row = lax.axis_index("row")
    col = lax.axis_index("col")
    positions = col * SLOTS + jnp.arange(SLOTS, dtype=jnp.int32)
    live = positions[None, :] < far_count[:, None]
    weighted = jnp.where(live[:, :, None, None], couplings, 0.0)
    weighted = weighted.transpose(0, 2, 1, 3).reshape(CL_DEV * RANK, SLOTS * RANK)
    owner = far_cols // CL_DEV
    core, rest = owner % NC, owner // NC
    tile = (
        ((row + NC - core) % NC) * (NY * NZ)
        + ((row // (NC * NZ) + NY - rest // NZ) % NY) * NZ
        + (row // NC + NZ - rest % NZ) % NZ
    )
    lists = jnp.concatenate(
        [tile * CL_DEV + far_cols % CL_DEV, near_cols - (row * CL_DEV - REACH)], axis=1
    ).astype(jnp.int32)
    lists = jnp.pad(lists, ((0, 8 - CL_DEV), (0, LANES - SLOTS - 1)))
    f32 = jnp.float32
    vmem = pl.BlockSpec(memory_space=pltpu.VMEM)
    dma = pltpu.SemaphoreType.DMA
    new_sol, hess = pl.pallas_call(
        kernel,
        out_shape=(
            jax.ShapeDtypeStruct((ROWS, LANES), f32),
            jax.ShapeDtypeStruct((24, LANES), f32),
        ),
        in_specs=[vmem] * 7,
        out_specs=(vmem, vmem),
        scratch_shapes=[
            pltpu.VMEM((SB + 1, ROWS, LANES), f32),
            pltpu.VMEM((SB, NC, NY, NZ, 8, LANES), f32),
            pltpu.VMEM((NROW * CL_DEV, RANK, LANES), f32),
            pltpu.VMEM((SB, NX, LANES, LANES), f32),
            pltpu.VMEM((SB, 2, LANES, LANES), f32),
            pltpu.VMEM((CL_DEV + 2 * REACH, LEAF_UNKNOWNS, LANES), f32),
            pltpu.VMEM((CL_DEV, FAR * RANK, LANES), f32),
            pltpu.VMEM((NX - 1, CL_DEV, LEAF_UNKNOWNS, LEAF_UNKNOWNS), f32),
            pltpu.VMEM((NX - 1, CL_DEV * RANK, SLOTS * RANK), f32),
            pltpu.VMEM((16, LANES), f32),
            pltpu.VMEM((NZ, 8, LANES), f32),
            pltpu.VMEM((NY, 8, LANES), f32),
            pltpu.VMEM((NC, 8, LANES), f32),
            pltpu.VMEM((SB - 1, ROWS, LANES), f32),
            pltpu.VMEM((NX, 24, LANES), f32),
            pltpu.VMEM((NX - 1, 8, LANES), jnp.int32),
            pltpu.SMEM((NX, 8, LANES), jnp.int32),
            dma((SB + 1,)), dma((SB + 1, len(RUNS))),
            dma((SB + 1, len(RUNS), NY - 1)), dma((SB + 1, len(RUNS), NY - 1)),
            dma((SB + 1, len(RUNS))), dma((SB + 1, len(RUNS))),
            dma((SB, 2)), dma((SB, 2)),
            dma((6,)), dma((6,)),
            dma((NX - 1,)), dma((NX - 1,)),
            dma((SB - 1, NX - 1)), dma((SB - 1, NX - 1)),
            dma((NX - 1,)), dma((NX - 1,)),
            dma((NX - 1,)), dma((NX - 1,)), dma((NX,)),
        ],
        compiler_params=pltpu.CompilerParams(
            collective_id=0, has_side_effects=True, vmem_limit_bytes=48 * 1024 * 1024
        ),
    )(
        lists,
        residual,
        solution,
        near_field_blocks.reshape(CL_DEV, LEAF_UNKNOWNS, LEAF_UNKNOWNS),
        weighted,
        col_basis,
        row_basis.transpose(0, 2, 1),
    )
    return (new_sol, hess[: (SB + 1) * SB].reshape(SB + 1, SB, LANES))


def solution(mesh):
    placed = (
        P("row", None),
        P("row", None),
        P("row", "col", None, None),
        P("row", "col"),
        P("row", "col", None, None),
        P("row", "col"),
        P("row"),
        P("row", None, None),
        P("row", None, None),
    )
    return jax.shard_map(
        local, mesh=mesh, in_specs=placed, out_specs=(P("row", None), P()), check_vma=False
    )
```
